32 devices in a mesh: section: 2 (over x), seq: 4 (over z), tensor: 4 (over y, core).
Axes of the slice: x: 2, y: 2, z: 4, core: 2. Of those that a mesh axis runs over, the one named last changes fastest.
Arguments:
- q_mant: bfloat16 [2, 256, 16384], P('section', 'seq', 'tensor'), may hold values from -32 to 32
- q_scale: int32 [2, 256, 512], P('section', 'seq', 'tensor'), may hold values from -2 to 2
- key_mantissa_block: bfloat16 [2, 256, 1024], P('section', 'seq', 'tensor'), may hold values from -32 to 32
- key_exponent_scale: int32 [2, 256, 32], P('section', 'seq', 'tensor'), may hold values from -2 to 2
- value_mantissa_block: bfloat16 [2, 256, 1024], P('section', 'seq', 'tensor'), may hold values from -6 to 6
- value_exponent_scale: int32 [2, 256, 32], P('section', 'seq', 'tensor'), may hold values from -1 to 1
- cached_key_rows: bfloat16 [2, 8, 512, 128], P('section', 'tensor', 'seq'), may hold values from -12 to 12
- cached_value_rows: bfloat16 [2, 8, 512, 128], P('section', 'tensor', 'seq'), may hold values from -8 to 8
- start: int32 [2], P('section'), may hold values from 256 to 512, as said below
Outputs:
- attended: bfloat16 [2, 256, 16384], P('section', 'seq', 'tensor')
The draws below stay inside these ranges and needn't reach their ends.
Inputs may be any that keep to these rules, and one draw needn't show every extreme that they name: The first start[s] cached positions of section s hold earlier tokens; the cache of some section is full in every draw.
All inputs are finite; a program needn't handle non-finite values.
Results may differ from the reference program's by a relative error of at most 0.0023.
Values may be sent and summed in bfloat16 or wider, within the bound.
No kernel may reach another device: no remote copies, remote signals or barrier semaphores. Data moves between devices by JAX's collectives and lax.ppermute only.
A program may use at most 64 MiB of HBM per device.

```python
import math
import jax
import jax.numpy as jnp
from jax import lax

QUERY_HEADS = 128
KEY_VALUE_HEADS = 8
HEAD_WIDTH = 128
RELAY_SECTIONS = 2
BLOCK_TOKENS = 256
CACHED_POSITIONS = 512


def exponent_lookup(key, feature_count):
    return jax.random.randint(key, (RELAY_SECTIONS, BLOCK_TOKENS, feature_count // 32), -2, 3, dtype=jnp.int32)


def draw_q_scale(key, part):
    return exponent_lookup(jax.random.fold_in(key, 101), QUERY_HEADS * HEAD_WIDTH)


def draw_key_exponent_scale(key, part):
    return exponent_lookup(jax.random.fold_in(key, 102), KEY_VALUE_HEADS * HEAD_WIDTH)


def mantissa_pair(key):
    q_base = jnp.clip(jax.random.normal(jax.random.fold_in(key, 211), (RELAY_SECTIONS, BLOCK_TOKENS, QUERY_HEADS * HEAD_WIDTH), jnp.float32), -6.0, 6.0)
    key_exponent_base = jnp.clip(jax.random.normal(jax.random.fold_in(key, 212), (RELAY_SECTIONS, BLOCK_TOKENS, KEY_VALUE_HEADS * HEAD_WIDTH), jnp.float32), -6.0, 6.0)
    return (q_base.astype(jnp.bfloat16), key_exponent_base.astype(jnp.bfloat16))


def draw_q_mant(key, part):
    return mantissa_pair(key)[0]


def draw_key_mantissa_block(key, part):
    return mantissa_pair(key)[1]


def draw_start(key, part):
    lowest = jax.random.randint(jax.random.fold_in(key, 301), (RELAY_SECTIONS,), CACHED_POSITIONS // 2, CACHED_POSITIONS + 1, dtype=jnp.int32)
    chosen = jax.random.randint(jax.random.fold_in(key, 302), (), 0, RELAY_SECTIONS, dtype=jnp.int32)
    return jnp.where(jnp.arange(RELAY_SECTIONS, dtype=jnp.int32) == chosen, CACHED_POSITIONS, lowest).astype(jnp.int32)


def touch_ends(values, stream_key, low, largest):
    longest = values.shape.index(max(values.shape))
    spots = []
    for shift in (0, 1):
        where = [jax.random.randint(jax.random.fold_in(stream_key, axis), (), 0, length) for axis, length in enumerate(values.shape)]
        where[longest] = (where[longest] + shift) % values.shape[longest]
        spots.append(tuple(where))
    return values.at[spots[0]].set(low).at[spots[1]].set(largest)


def steps_of(rng, dims, cuts, least, high):
    factor_of, own = 1.0, jax.random.fold_in(rng, 6)
    for position, blocks in cuts:
        steps = jnp.exp(jax.random.uniform(jax.random.fold_in(own, position), (blocks,), jnp.float32, least / len(cuts), high / len(cuts)))
        factor_of = factor_of * jnp.repeat(steps, dims[position] // blocks).reshape([-1 if axis == position else 1 for axis in range(len(dims))])
    return factor_of


def gaussian(own_key, extent, scale, reach, pieces=(), held_as=jnp.bfloat16):
    drawn = scale * jax.random.normal(own_key, extent, jnp.float32)
    if pieces:
        drawn = drawn * steps_of(own_key, extent, pieces, -0.22, 0.18)
    return jnp.clip(drawn, -reach, reach).astype(held_as)


def setup_inputs(seed: int = 0) -> dict:
    streams_of = jax.random.split(jax.random.key(seed), 10)
    return {
        "q_mant": draw_q_mant(jax.random.fold_in(streams_of[9], 71), 0),
        "q_scale": draw_q_scale(jax.random.fold_in(streams_of[9], 71), 0),
        "key_mantissa_block": draw_key_mantissa_block(jax.random.fold_in(streams_of[9], 71), 0),
        "key_exponent_scale": draw_key_exponent_scale(jax.random.fold_in(streams_of[9], 71), 0),
        "value_mantissa_block": gaussian(streams_of[4], (RELAY_SECTIONS, BLOCK_TOKENS, KEY_VALUE_HEADS * HEAD_WIDTH), 1.0, 6.0, ((0, 2), (1, 4), (2, 4))),
        "value_exponent_scale": touch_ends(jax.random.randint(streams_of[5], (RELAY_SECTIONS, BLOCK_TOKENS, KEY_VALUE_HEADS * HEAD_WIDTH // 32), -1, 2), jax.random.fold_in(streams_of[5], 1), -1, 1).astype(jnp.int32),
        "cached_key_rows": gaussian(streams_of[6], (RELAY_SECTIONS, KEY_VALUE_HEADS, CACHED_POSITIONS, HEAD_WIDTH), 2.0, 12.0, ((0, 2), (1, 4), (2, 4))),
        "cached_value_rows": gaussian(streams_of[7], (RELAY_SECTIONS, KEY_VALUE_HEADS, CACHED_POSITIONS, HEAD_WIDTH), 1.3, 8.0, ((0, 2), (1, 4), (2, 4))),
        "start": draw_start(jax.random.fold_in(streams_of[9], 71), 0),
    }


def decode_mantissas(mantissa, exponent):
    row_count, feature_count = mantissa.shape
    blocks = mantissa.astype(jnp.float32).reshape(row_count, feature_count // 32, 32)
    factor = jnp.exp2(exponent.astype(jnp.float32))[:, :, None]
    return (blocks * factor).reshape(row_count, feature_count).astype(jnp.bfloat16)

def reference(q_mant, q_scale, key_mantissa_block, key_exponent_scale, value_mantissa_block, value_exponent_scale, cached_key_rows, cached_value_rows, start):
    query_group_width = QUERY_HEADS // KEY_VALUE_HEADS
    inv_root = 1.0 / math.sqrt(HEAD_WIDTH)
    results = []
    for section_index in range(RELAY_SECTIONS):
        sender_section = (section_index - 1) % RELAY_SECTIONS
        queries = decode_mantissas(q_mant[sender_section], q_scale[sender_section]).reshape(BLOCK_TOKENS, QUERY_HEADS, HEAD_WIDTH)
        section_key_rows = decode_mantissas(key_mantissa_block[sender_section], key_exponent_scale[sender_section]).reshape(BLOCK_TOKENS, KEY_VALUE_HEADS, HEAD_WIDTH)
        section_value_rows = decode_mantissas(value_mantissa_block[sender_section], value_exponent_scale[sender_section]).reshape(BLOCK_TOKENS, KEY_VALUE_HEADS, HEAD_WIDTH)
        all_keys = jnp.concatenate([cached_key_rows[section_index], jnp.transpose(section_key_rows, (1, 0, 2))], axis=1)
        all_values = jnp.concatenate([cached_value_rows[section_index], jnp.transpose(section_value_rows, (1, 0, 2))], axis=1)
        cache_pos = jnp.arange(CACHED_POSITIONS, dtype=jnp.int32)
        query_pos = jnp.arange(BLOCK_TOKENS, dtype=jnp.int32)
        cache_ok = jnp.broadcast_to((cache_pos < start[section_index])[None, :], (BLOCK_TOKENS, CACHED_POSITIONS))
        span_ok = query_pos[None, :] <= query_pos[:, None]
        allowed = jnp.concatenate([cache_ok, span_ok], axis=1)

        def one_head(head_index):
            kv_head = head_index // query_group_width
            query_rows = lax.dynamic_index_in_dim(queries, head_index, 1, keepdims=False).astype(jnp.float32)
            head_keys = lax.dynamic_index_in_dim(all_keys, kv_head, 0, keepdims=False).astype(jnp.float32)
            head_values = lax.dynamic_index_in_dim(all_values, kv_head, 0, keepdims=False).astype(jnp.float32)
            scores = jnp.dot(query_rows, head_keys.T, preferred_element_type=jnp.float32) * inv_root
            scores = jnp.where(allowed, scores, -jnp.inf)
            row_max = lax.optimization_barrier(jnp.max(scores, axis=1, keepdims=True))
            weights = jnp.where(allowed, jnp.exp(scores - row_max), 0.0)
            row_total = lax.optimization_barrier(jnp.sum(weights, axis=1))
            rounded = lax.optimization_barrier(weights.astype(jnp.bfloat16)).astype(jnp.float32)
            mixed = jnp.dot(rounded, head_values, preferred_element_type=jnp.float32)
            return (mixed / row_total[:, None]).astype(jnp.bfloat16)
        heads_out = lax.map(one_head, jnp.arange(QUERY_HEADS, dtype=jnp.int32))
        results.append(jnp.transpose(heads_out, (1, 0, 2)).reshape(BLOCK_TOKENS, QUERY_HEADS * HEAD_WIDTH))
    return jnp.stack(results, axis=0)
```

```python
import functools
import math

import jax
import jax.numpy as jnp
from jax import lax
from jax.experimental import pallas as pl
from jax.experimental.pallas import tpu as pltpu
from jax.sharding import PartitionSpec as P

NEG = -1e30
VMEM = pltpu.MemorySpace.VMEM


def spread(scale, first, width):
    lanes = lax.broadcasted_iota(jnp.int32, scale.shape, 1)
    return jnp.take_along_axis(scale, first + lanes // 32, axis=1)


def pack_kernel(start_ref, km_ref, ks_ref, vm_ref, vs_ref, qs_ref, ck_ref, cv_ref, kv_ref, sc_ref, c_ref, bias_ref, *, count, width):
    kv_heads = ck_ref.shape[1]
    per = width // 32
    rows = km_ref.shape[1]
    pad = jnp.zeros((rows, width - ks_ref.shape[2]), jnp.float32)
    for part, (mant, exponent) in enumerate(((km_ref, ks_ref), (vm_ref, vs_ref))):
        scale = jnp.concatenate([jnp.exp2(exponent[0].astype(jnp.float32)), pad], axis=1)
        for g in range(kv_heads):
            cols = pl.ds(g * width, width)
            value = mant[0, :, cols].astype(jnp.float32) * spread(scale, g * per, width)
            kv_ref[:, pl.ds((part * kv_heads + g) * width, width)] = value.astype(jnp.bfloat16)
    sc_ref[...] = qs_ref[0].astype(jnp.float32).astype(jnp.bfloat16)
    for g in range(kv_heads):
        c_ref[g] = ck_ref[0, g]
        c_ref[kv_heads + g] = cv_ref[0, g]
    here = lax.axis_index("seq")
    held = ck_ref.shape[2]
    shape = (held, width)
    key = lax.broadcasted_iota(jnp.int32, shape, 0)
    for d in range(count):
        source = lax.rem(here - d + count, count)
        bias_ref[pl.ds(d * held, held), :] = jnp.where(source * held + key < start_ref[0], 0.0, NEG).astype(jnp.bfloat16)
    shape = (rows, width)
    key = lax.broadcasted_iota(jnp.int32, shape, 0)
    token = lax.broadcasted_iota(jnp.int32, shape, 1)
    for d in range(count):
        source = lax.rem(here - d + count, count)
        bias_ref[pl.ds(count * held + d * rows, rows), :] = jnp.where(
            source * rows + key <= here * rows + token, 0.0, NEG
        ).astype(jnp.bfloat16)


def attend_kernel(*refs, count, kv_heads, width, group):
    q_ref, sc_ref, bias_ref = refs[:3]
    c_refs = refs[3 : 3 + count]
    b_refs = refs[3 + count : 3 + 2 * count]
    out_ref = refs[3 + 2 * count]
    k_all, v_all, staged, sem = refs[4 + 2 * count :]
    rows = q_ref.shape[0]
    held = c_refs[0].shape[1]
    heads = q_ref.shape[1] // width
    per_kv = heads // kv_heads
    per = width // 32
    factor = math.log2(math.e) / math.sqrt(width)
    for g in range(kv_heads):
        for d in range(count):
            k_all[g, pl.ds(d * held, held), pl.ds(0, width)] = c_refs[d][g]
            v_all[g, pl.ds(d * held, held), :] = c_refs[d][kv_heads + g]
            at = pl.ds(count * held + d * rows, rows)
            k_all[g, at, pl.ds(0, width)] = b_refs[d][:, pl.ds(g * width, width)]
            v_all[g, at, :] = b_refs[d][:, pl.ds((kv_heads + g) * width, width)]
        k_all[g, :, pl.ds(width, width)] = bias_ref[...]
    scale = jnp.exp2(sc_ref[...].astype(jnp.float32))
    mark = jnp.where(
        lax.broadcasted_iota(jnp.int32, (rows, width), 0)
        == lax.broadcasted_iota(jnp.int32, (rows, width), 1),
        1.0,
        0.0,
    ).astype(jnp.bfloat16)
    copies = []
    for step in range(heads // group):
        g = step * group // per_kv
        blocks = []
        for k in range(group):
            head = step * group + k
            value = q_ref[:, pl.ds(head * width, width)].astype(jnp.float32)
            value = (value * spread(scale, head * per, width)).astype(jnp.bfloat16)
            blocks.append(jnp.concatenate([value, mark], axis=1))
        q = jnp.concatenate(blocks, axis=0)
        s = lax.dot_general(q, k_all[g], (((1,), (1,)), ((), ())), preferred_element_type=jnp.float32)
        top = jnp.max(s, axis=1, keepdims=True)
        w = jnp.exp2((s - top) * factor)
        total = jnp.sum(w, axis=1, keepdims=True)
        o = jnp.dot(w.astype(jnp.bfloat16), v_all[g], preferred_element_type=jnp.float32)
        o = (o / total).astype(jnp.bfloat16)
        for k in range(group):
            staged[:, pl.ds((step * group + k) * width, width)] = o[k * rows : (k + 1) * rows]
        cols = pl.ds(step * group * width, group * width)
        copy = pltpu.make_async_copy(staged.at[:, cols], out_ref.at[0, :, cols], sem.at[step])
        copy.start()
        copies.append(copy)
    for copy in copies:
        copy.wait()


def shift(x, axis, distance):
    size = lax.axis_size(axis)
    return lax.ppermute(x, axis, [(i, (i + distance) % size) for i in range(size)])


def vmem():
    return pl.BlockSpec(memory_space=VMEM)


def body(q_mant, q_scale, key_m, key_e, value_m, value_e, cached_k, cached_v, start):
    _, rows, features = q_mant.shape
    _, kv_heads, held, width = cached_k.shape
    count = lax.axis_size("seq")
    heads = features // width
    keys = count * (held + rows)
    bf16 = jnp.bfloat16
    kv, sc, cached, bias = pl.pallas_call(
        functools.partial(pack_kernel, count=count, width=width),
        out_shape=(
            jax.ShapeDtypeStruct((rows, 2 * kv_heads * width), bf16),
            jax.ShapeDtypeStruct((rows, q_scale.shape[2]), bf16),
            jax.ShapeDtypeStruct((2 * kv_heads, held, width), bf16),
            jax.ShapeDtypeStruct((keys, width), bf16),
        ),
        in_specs=[pl.BlockSpec(memory_space=pltpu.SMEM)] + [vmem()] * 7,
        out_specs=(vmem(),) * 4,
        name="pack",
    )(start, key_m, key_e, value_m, value_e, q_scale, cached_k, cached_v)
    kv = shift(kv, "section", 1)
    sc = shift(sc, "section", 1)
    q = shift(q_mant[0], "section", 1)
    if count <= 4:
        c = [cached] + [shift(cached, "seq", d) for d in range(1, count)]
        b = [kv] + [shift(kv, "seq", d) for d in range(1, count)]
    else:
        here = lax.axis_index("seq")
        order = (here - jnp.arange(count)) % count
        c = lax.all_gather(cached, "seq", axis=0)[order]
        b = lax.all_gather(kv, "seq", axis=0)[order]
        c = [c[d] for d in range(count)]
        b = [b[d] for d in range(count)]
    group = 4
    return pl.pallas_call(
        functools.partial(attend_kernel, count=count, kv_heads=kv_heads, width=width, group=group),
        out_shape=jax.ShapeDtypeStruct((1, rows, features), bf16),
        in_specs=[vmem()] * (3 + 2 * count),
        out_specs=pl.BlockSpec(memory_space=pl.ANY),
        scratch_shapes=[
            pltpu.VMEM((kv_heads, keys, 2 * width), bf16),
            pltpu.VMEM((kv_heads, keys, width), bf16),
            pltpu.VMEM((rows, features), bf16),
            pltpu.SemaphoreType.DMA((heads // group,)),
        ],
        name="attend",
    )(q, sc, bias, *c, *b)


def solution(mesh):
    rows = P("section", "seq", "tensor")
    return jax.shard_map(
        body,
        mesh=mesh,
        in_specs=(rows,) * 6 + (P("section", "tensor", "seq", None),) * 2 + (P("section"),),
        out_specs=rows,
        check_vma=False,
    )
```

```python
import functools
import math

import jax
import jax.numpy as jnp
from jax import lax
from jax.experimental import pallas as pl
from jax.experimental.pallas import tpu as pltpu
from jax.sharding import PartitionSpec as P


NEG = -1e30
VMEM = pl.BlockSpec(memory_space=pltpu.MemorySpace.VMEM)
HBM = pl.BlockSpec(memory_space=pltpu.MemorySpace.HBM)
BLOCK = 32
bf16, f32 = jnp.bfloat16, jnp.float32


def spread(scale, first):
    lanes = lax.broadcasted_iota(jnp.int32, scale.shape, 1)
    return jnp.take_along_axis(scale, first + lanes // BLOCK, axis=1)


def decoded(mantissa, scale, first):
    return (mantissa.astype(f32) * spread(scale, first)).astype(bf16)


def first_kernel(qs, km, ks, vm, vs, ck, cv, kv_ref, c_ref, qsb, kmb, ksb, vmb, vsb, sem, *, width):
    _, kv_heads, _, _ = ck.shape
    rows = kv_ref.shape[0]
    pairs = (
        (qs.at[0], qsb),
        (ks.at[0], ksb),
        (vs.at[0], vsb),
        (km.at[0], kmb),
        (vm.at[0], vmb),
        (ck.at[0], c_ref.at[pl.ds(0, kv_heads)]),
        (cv.at[0], c_ref.at[pl.ds(kv_heads, kv_heads)]),
    )
    copies = [pltpu.make_async_copy(a, b, sem.at[i]) for i, (a, b) in enumerate(pairs)]
    for copy in copies:
        copy.start()
    for copy in copies[:5]:
        copy.wait()
    per = width // BLOCK
    pad = jnp.zeros((width - ksb.shape[0], rows), f32)
    for part, (mant, exponent) in enumerate(((kmb, ksb), (vmb, vsb))):
        scale = jnp.concatenate([jnp.exp2(exponent[...].astype(f32)), pad], axis=0).T
        for g in range(kv_heads):
            kv_ref[:, pl.ds((part * kv_heads + g) * width, width)] = decoded(mant[:, pl.ds(g * width, width)], scale, g * per)
    kv_ref[:, pl.ds(2 * kv_heads * width, qsb.shape[1])] = qsb[...].astype(f32).astype(bf16)
    for copy in copies[5:]:
        copy.wait()


def bias_kernel(start, bias_ref, at, sem, *, count, held, rows, source):
    width = bias_ref.shape[1]
    copy = pltpu.make_async_copy(start, at, sem)
    copy.start()
    here = lax.axis_index("seq")
    key = lax.broadcasted_iota(jnp.int32, (rows, width), 0)
    token = lax.broadcasted_iota(jnp.int32, (rows, width), 1)
    for d in range(count):
        bias_ref[pl.ds(count * held + d * rows, rows), :] = jnp.where(
            source(here, d) * rows + key <= here * rows + token, 0.0, NEG
        ).astype(bf16)
    copy.wait()
    key = lax.broadcasted_iota(jnp.int32, (held, width), 0)
    for d in range(count):
        bias_ref[pl.ds(d * held, held), :] = jnp.where(source(here, d) * held + key < at[0], 0.0, NEG).astype(bf16)


def attend_kernel(*refs, cs, bs, pick, kv_heads, width, group):
    q_ref, sc_ref, bias_ref = refs[:3]
    c_refs = refs[3 : 3 + cs]
    b_refs = refs[3 + cs : 3 + cs + bs]
    out_ref, k_all, v_all, staged, sem = refs[3 + cs + bs :]
    rows = q_ref.shape[0]
    held = c_refs[0].shape[-2]
    heads = out_ref.shape[2] // width
    per_kv = heads // kv_heads
    factor = math.log2(math.e) / math.sqrt(width)
    c_keys, c_values, blocks_kv = pick(c_refs, b_refs)
    count = len(c_keys)
    for g in range(kv_heads):
        for d in range(count):
            k_all[g, pl.ds(d * held, held), pl.ds(0, width)] = c_keys[d](g)
            v_all[g, pl.ds(d * held, held), :] = c_values[d](g)
            at = pl.ds(count * held + d * rows, rows)
            k_all[g, at, pl.ds(0, width)] = blocks_kv[d][:, pl.ds(g * width, width)]
            v_all[g, at, :] = blocks_kv[d][:, pl.ds((kv_heads + g) * width, width)]
        k_all[g, :, pl.ds(width, width)] = bias_ref[...]
    mark = jnp.where(
        lax.broadcasted_iota(jnp.int32, (rows, width), 0) == lax.broadcasted_iota(jnp.int32, (rows, width), 1),
        1.0,
        0.0,
    ).astype(bf16)
    scale = jnp.exp2(sc_ref[...].astype(f32))
    per = width // BLOCK
    copies = []

    def scores(step):
        g = step * group // per_kv
        blocks = []
        for k in range(group):
            head = step * group + k
            value = decoded(q_ref[:, pl.ds(head * width, width)], scale, head * per)
            blocks.append(jnp.concatenate([value, mark], axis=1))
        return lax.dot_general(jnp.concatenate(blocks, axis=0), k_all[g], (((1,), (1,)), ((), ())), preferred_element_type=f32)

    steps = heads // group
    s = scores(0)
    for step in range(steps):
        g = step * group // per_kv
        later = scores(step + 1) if step + 1 < steps else None
        top = jnp.max(s, axis=1, keepdims=True)
        w = jnp.exp2((s - top) * factor)
        total = jnp.sum(w, axis=1, keepdims=True)
        o = jnp.dot(w.astype(bf16), v_all[g], preferred_element_type=f32)
        o = (o / total).astype(bf16)
        s = later
        for k in range(group):
            staged[:, pl.ds((step * group + k) * width, width)] = o[k * rows : (k + 1) * rows]
        cols = pl.ds(step * group * width, group * width)
        copy = pltpu.make_async_copy(staged.at[:, cols], out_ref.at[0, :, cols], sem.at[step])
        copy.start()
        copies.append(copy)
    for copy in copies:
        copy.wait()


def natural(here, d):
    return jnp.int32(d)


def mirrored(here, d):
    return lax.bitwise_xor(here, d)


NEAR = [(0, 1), (1, 0), (2, 3), (3, 2)]
FAR = [(0, 2), (2, 0), (1, 3), (3, 1)]


def pick_natural(c_refs, b_refs):
    c, b = c_refs[0], b_refs[0]
    count = c.shape[0]
    kv_heads = c.shape[1] // 2
    keys = [lambda g, d=d: c[d, g] for d in range(count)]
    values = [lambda g, d=d: c[d, kv_heads + g] for d in range(count)]
    return keys, values, [b.at[d] for d in range(count)]


def pick_mirrored(c_refs, b_refs):
    kv_heads = c_refs[0].shape[0] // 2
    keys = [lambda g, c=c: c[g] for c in c_refs]
    values = [lambda g, c=c: c[kv_heads + g] for c in c_refs]
    return keys, values, b_refs


def body(q_mant, q_scale, key_m, key_e, value_m, value_e, cached_k, cached_v, start):
    _, rows, features = q_mant.shape
    _, kv_heads, held, width = cached_k.shape
    count = lax.axis_size("seq")
    sections = lax.axis_size("section")
    heads = features // width
    keys = count * (held + rows)
    mirror = count == len(NEAR)
    kv, cached = pl.pallas_call(
        functools.partial(first_kernel, width=width),
        out_shape=(
            jax.ShapeDtypeStruct((rows, 2 * kv_heads * width + q_scale.shape[2]), bf16),
            jax.ShapeDtypeStruct((2 * kv_heads, held, width), bf16),
        ),
        in_specs=[HBM] * 7,
        out_specs=(VMEM,) * 2,
        scratch_shapes=[
            pltpu.VMEM(q_scale.shape[1:], jnp.int32),
            pltpu.VMEM(key_m.shape[1:], bf16),
            pltpu.VMEM((key_e.shape[2], rows), jnp.int32),
            pltpu.VMEM(value_m.shape[1:], bf16),
            pltpu.VMEM((value_e.shape[2], rows), jnp.int32),
            pltpu.SemaphoreType.DMA((7,)),
        ],
        compiler_params=pltpu.CompilerParams(vmem_limit_bytes=60 << 20),
        name="first",
    )(q_scale, key_m, jnp.swapaxes(key_e, 1, 2), value_m, jnp.swapaxes(value_e, 1, 2), cached_k, cached_v)
    bias = pl.pallas_call(
        functools.partial(bias_kernel, count=count, held=held, rows=rows, source=mirrored if mirror else natural),
        out_shape=jax.ShapeDtypeStruct((keys, width), bf16),
        in_specs=[HBM],
        out_specs=VMEM,
        scratch_shapes=[pltpu.SMEM((1,), jnp.int32), pltpu.SemaphoreType.DMA],
        compiler_params=pltpu.CompilerParams(vmem_limit_bytes=8 << 20),
        name="bias",
    )(start)
    relay = [(i, (i + 1) % sections) for i in range(sections)]
    kv = lax.ppermute(kv, "section", relay)
    kv, scale = kv[:, : 2 * kv_heads * width], kv[:, 2 * kv_heads * width :]
    q = lax.ppermute(q_mant[0], "section", relay)
    if mirror:
        near = lax.ppermute(cached, "seq", NEAR)
        far = lax.ppermute(cached, "seq", FAR)
        c = [cached, near, far, lax.ppermute(far, "seq", NEAR)]
        far = lax.ppermute(kv, "seq", FAR)
        near = lax.ppermute(kv, "seq", NEAR)
        b = [kv, near, far, lax.ppermute(far, "seq", NEAR)]
    else:
        c = [lax.all_gather(cached, "seq", axis=0)]
        b = [lax.all_gather(kv, "seq", axis=0)]
    group = 4
    limit = (8 << 20) + keys * width * kv_heads * 8 + keys * group * rows * 12 + 4 * rows * features
    return pl.pallas_call(
        functools.partial(
            attend_kernel,
            cs=len(c),
            bs=len(b),
            pick=pick_mirrored if mirror else pick_natural,
            kv_heads=kv_heads,
            width=width,
            group=group,
        ),
        out_shape=jax.ShapeDtypeStruct((1, rows, features), bf16),
        in_specs=[VMEM] * (3 + len(c) + len(b)),
        out_specs=pl.BlockSpec(memory_space=pl.ANY),
        scratch_shapes=[
            pltpu.VMEM((kv_heads, keys, 2 * width), bf16),
            pltpu.VMEM((kv_heads, keys, width), bf16),
            pltpu.VMEM((rows, features), bf16),
            pltpu.SemaphoreType.DMA((heads // group,)),
        ],
        compiler_params=pltpu.CompilerParams(vmem_limit_bytes=limit),
        name="attend",
    )(q, scale, bias, *c, *b)


def solution(mesh):
    rows = P("section", "seq", "tensor")

    return jax.shard_map(
        body,
        mesh=mesh,
        in_specs=(rows,) * 6 + (P("section", "tensor", "seq", None),) * 2 + (P("section"),),
        out_specs=rows,
        check_vma=False,
    )
```

```python
import functools
import math

import jax
import jax.numpy as jnp
from jax import lax
from jax.experimental import pallas as pl
from jax.experimental.pallas import tpu as pltpu
from jax.sharding import PartitionSpec as P


NEG = -1e30
VMEM = pl.BlockSpec(memory_space=pltpu.MemorySpace.VMEM)
HBM = pl.BlockSpec(memory_space=pltpu.MemorySpace.HBM)
BLOCK = 32
bf16, f32 = jnp.bfloat16, jnp.float32


def spread(scale, first):
    lanes = lax.broadcasted_iota(jnp.int32, scale.shape, 1)
    return jnp.take_along_axis(scale, first + lanes // BLOCK, axis=1)


def decoded(mantissa, scale, first):
    return (mantissa.astype(f32) * spread(scale, first)).astype(bf16)


def first_kernel(qs, km, ks, vm, vs, ck, cv, kv_ref, c_ref, qsb, kmb, ksb, vmb, vsb, sem, *, width):
    _, kv_heads, _, _ = ck.shape
    rows = kv_ref.shape[0]
    pairs = (
        (qs.at[0], qsb),
        (ks.at[0], ksb),
        (vs.at[0], vsb),
        (km.at[0], kmb),
        (vm.at[0], vmb),
        (ck.at[0], c_ref.at[pl.ds(0, kv_heads)]),
        (cv.at[0], c_ref.at[pl.ds(kv_heads, kv_heads)]),
    )
    copies = [pltpu.make_async_copy(a, b, sem.at[i]) for i, (a, b) in enumerate(pairs)]
    for copy in copies:
        copy.start()
    for copy in copies[:5]:
        copy.wait()
    per = width // BLOCK
    pad = jnp.zeros((width - ksb.shape[0], rows), f32)
    for part, (mant, exponent) in enumerate(((kmb, ksb), (vmb, vsb))):
        scale = jnp.concatenate([jnp.exp2(exponent[...].astype(f32)), pad], axis=0).T
        for g in range(kv_heads):
            kv_ref[:, pl.ds((part * kv_heads + g) * width, width)] = decoded(mant[:, pl.ds(g * width, width)], scale, g * per)
    kv_ref[:, pl.ds(2 * kv_heads * width, qsb.shape[1])] = qsb[...].astype(f32).astype(bf16)
    for copy in copies[5:]:
        copy.wait()


def bias_kernel(start, bias_ref, at, sem, *, count, held, rows, source):
    width = bias_ref.shape[1]
    copy = pltpu.make_async_copy(start, at, sem)
    copy.start()
    here = lax.axis_index("seq")
    key = lax.broadcasted_iota(jnp.int32, (rows, width), 0)
    token = lax.broadcasted_iota(jnp.int32, (rows, width), 1)
    for d in range(count):
        bias_ref[pl.ds(count * held + d * rows, rows), :] = jnp.where(
            source(here, d) * rows + key <= here * rows + token, 0.0, NEG
        ).astype(bf16)
    copy.wait()
    key = lax.broadcasted_iota(jnp.int32, (held, width), 0)
    for d in range(count):
        bias_ref[pl.ds(d * held, held), :] = jnp.where(source(here, d) * held + key < at[0], 0.0, NEG).astype(bf16)


def attend_kernel(*refs, cs, bs, pick, kv_heads, width, group):
    q_ref, sc_ref, bias_ref = refs[:3]
    c_refs = refs[3 : 3 + cs]
    b_refs = refs[3 + cs : 3 + cs + bs]
    out_ref, k_all, v_all, staged, sem = refs[3 + cs + bs :]
    rows = q_ref.shape[0]
    held = c_refs[0].shape[-2]
    heads = out_ref.shape[2] // width
    per_kv = heads // kv_heads
    factor = math.log2(math.e) / math.sqrt(width)
    c_keys, c_values, blocks_kv = pick(c_refs, b_refs)
    count = len(c_keys)
    for g in range(kv_heads):
        for d in range(count):
            k_all[g, pl.ds(d * held, held), pl.ds(0, width)] = c_keys[d](g)
            v_all[g, pl.ds(d * held, held), :] = c_values[d](g)
            at = pl.ds(count * held + d * rows, rows)
            k_all[g, at, pl.ds(0, width)] = blocks_kv[d][:, pl.ds(g * width, width)]
            v_all[g, at, :] = blocks_kv[d][:, pl.ds((kv_heads + g) * width, width)]
        k_all[g, :, pl.ds(width, width)] = bias_ref[...]
    mark = jnp.where(
        lax.broadcasted_iota(jnp.int32, (rows, width), 0) == lax.broadcasted_iota(jnp.int32, (rows, width), 1),
        1.0,
        0.0,
    ).astype(bf16)
    scale = jnp.exp2(sc_ref[...].astype(f32))
    per = width // BLOCK
    copies = []

    def scores(step):
        g = step * group // per_kv
        blocks = []
        for k in range(group):
            head = step * group + k
            value = decoded(q_ref[:, pl.ds(head * width, width)], scale, head * per)
            blocks.append(jnp.concatenate([value, mark], axis=1))
        return lax.dot_general(jnp.concatenate(blocks, axis=0), k_all[g], (((1,), (1,)), ((), ())), preferred_element_type=f32)

    steps = heads // group
    s = scores(0)
    for step in range(steps):
        g = step * group // per_kv
        later = scores(step + 1) if step + 1 < steps else None
        top = jnp.max(s, axis=1, keepdims=True)
        w = jnp.exp2((s - top) * factor)
        total = jnp.sum(w, axis=1, keepdims=True)
        o = jnp.dot(w.astype(bf16), v_all[g], preferred_element_type=f32)
        o = (o / total).astype(bf16)
        s = later
        for k in range(group):
            staged[:, pl.ds((step * group + k) * width, width)] = o[k * rows : (k + 1) * rows]
        cols = pl.ds(step * group * width, group * width)
        copy = pltpu.make_async_copy(staged.at[:, cols], out_ref.at[0, :, cols], sem.at[step])
        copy.start()
        copies.append(copy)
    for copy in copies:
        copy.wait()


def in_hbm(x):
    return pltpu.with_memory_space_constraint(x, pltpu.MemorySpace.HBM)


def natural(here, d):
    return jnp.int32(d)


def mirrored(here, d):
    return lax.bitwise_xor(here, d)


NEAR = [(0, 1), (1, 0), (2, 3), (3, 2)]
FAR = [(0, 2), (2, 0), (1, 3), (3, 1)]


def pick_natural(c_refs, b_refs):
    c, b = c_refs[0], b_refs[0]
    count = c.shape[0]
    kv_heads = c.shape[1] // 2
    keys = [lambda g, d=d: c[d, g] for d in range(count)]
    values = [lambda g, d=d: c[d, kv_heads + g] for d in range(count)]
    return keys, values, [b.at[d] for d in range(count)]


def pick_mirrored(c_refs, b_refs):
    kv_heads = c_refs[0].shape[0] // 2
    keys = [lambda g, c=c: c[g] for c in c_refs]
    values = [lambda g, c=c: c[kv_heads + g] for c in c_refs]
    return keys, values, b_refs


def body(q_mant, q_scale, key_m, key_e, value_m, value_e, cached_k, cached_v, start):
    _, rows, features = q_mant.shape
    _, kv_heads, held, width = cached_k.shape
    count = lax.axis_size("seq")
    sections = lax.axis_size("section")
    heads = features // width
    keys = count * (held + rows)
    mirror = count == len(NEAR)
    kv, cached = pl.pallas_call(
        functools.partial(first_kernel, width=width),
        out_shape=(
            jax.ShapeDtypeStruct((rows, 2 * kv_heads * width + q_scale.shape[2]), bf16),
            jax.ShapeDtypeStruct((2 * kv_heads, held, width), bf16),
        ),
        in_specs=[HBM] * 7,
        out_specs=(VMEM,) * 2,
        scratch_shapes=[
            pltpu.VMEM(q_scale.shape[1:], jnp.int32),
            pltpu.VMEM(key_m.shape[1:], bf16),
            pltpu.VMEM((key_e.shape[2], rows), jnp.int32),
            pltpu.VMEM(value_m.shape[1:], bf16),
            pltpu.VMEM((value_e.shape[2], rows), jnp.int32),
            pltpu.SemaphoreType.DMA((7,)),
        ],
        compiler_params=pltpu.CompilerParams(vmem_limit_bytes=8 << 20),
        name="first",
    )(*(
        in_hbm(x)
        for x in (q_scale, key_m, jnp.swapaxes(key_e, 1, 2), value_m, jnp.swapaxes(value_e, 1, 2), cached_k, cached_v)
    ))
    bias = pl.pallas_call(
        functools.partial(bias_kernel, count=count, held=held, rows=rows, source=mirrored if mirror else natural),
        out_shape=jax.ShapeDtypeStruct((keys, width), bf16),
        in_specs=[HBM],
        out_specs=VMEM,
        scratch_shapes=[pltpu.SMEM((1,), jnp.int32), pltpu.SemaphoreType.DMA],
        compiler_params=pltpu.CompilerParams(vmem_limit_bytes=8 << 20),
        name="bias",
    )(start)
    relay = [(i, (i + 1) % sections) for i in range(sections)]
    kv = lax.ppermute(kv, "section", relay)
    kv, scale = kv[:, : 2 * kv_heads * width], kv[:, 2 * kv_heads * width :]
    q = lax.ppermute(q_mant[0], "section", relay)
    if mirror:
        near = lax.ppermute(cached, "seq", NEAR)
        far = lax.ppermute(cached, "seq", FAR)
        c = [cached, near, far, lax.ppermute(far, "seq", NEAR)]
        far = lax.ppermute(kv, "seq", FAR)
        near = lax.ppermute(kv, "seq", NEAR)
        b = [kv, near, far, lax.ppermute(far, "seq", NEAR)]
    else:
        c = [lax.all_gather(cached, "seq", axis=0)]
        b = [lax.all_gather(kv, "seq", axis=0)]
    group = 4
    limit = (8 << 20) + keys * width * kv_heads * 8 + keys * group * rows * 12 + 4 * rows * features
    return pl.pallas_call(
        functools.partial(
            attend_kernel,
            cs=len(c),
            bs=len(b),
            pick=pick_mirrored if mirror else pick_natural,
            kv_heads=kv_heads,
            width=width,
            group=group,
        ),
        out_shape=jax.ShapeDtypeStruct((1, rows, features), bf16),
        in_specs=[VMEM] * (3 + len(c) + len(b)),
        out_specs=pl.BlockSpec(memory_space=pl.ANY),
        scratch_shapes=[
            pltpu.VMEM((kv_heads, keys, 2 * width), bf16),
            pltpu.VMEM((kv_heads, keys, width), bf16),
            pltpu.VMEM((rows, features), bf16),
            pltpu.SemaphoreType.DMA((heads // group,)),
        ],
        compiler_params=pltpu.CompilerParams(vmem_limit_bytes=limit),
        name="attend",
    )(q, scale, bias, *c, *b)


def solution(mesh):
    rows = P("section", "seq", "tensor")

    step = jax.shard_map(
        body,
        mesh=mesh,
        in_specs=(rows,) * 6 + (P("section", "tensor", "seq", None),) * 2 + (P("section"),),
        out_specs=rows,
        check_vma=False,
    )
    if mesh.shape["seq"] != len(NEAR):
        return step
    return step
```

```python
import functools
import math

import jax
import jax.numpy as jnp
from jax import lax
from jax.experimental import pallas as pl
from jax.experimental.pallas import tpu as pltpu
from jax.sharding import PartitionSpec as P


NEG = -1e30
VMEM = pl.BlockSpec(memory_space=pltpu.MemorySpace.VMEM)
HBM = pl.BlockSpec(memory_space=pltpu.MemorySpace.HBM)
BLOCK = 32
bf16, f32 = jnp.bfloat16, jnp.float32


def spread(scale, first):
    lanes = lax.broadcasted_iota(jnp.int32, scale.shape, 1)
    return jnp.take_along_axis(scale, first + lanes // BLOCK, axis=1)


def decoded(mantissa, scale, first):
    return (mantissa.astype(f32) * spread(scale, first)).astype(bf16)


def first_kernel(*refs, width):
    q, qs, km, ks, vm, vs, ck, cv, kv_ref, c_ref = refs[:10]
    q_refs = refs[10:-6]
    qsb, kmb, ksb, vmb, vsb, sem = refs[-6:]
    _, kv_heads, _, _ = ck.shape
    rows = kv_ref.shape[0]
    pairs = [
        (qs.at[0], qsb),
        (ks.at[0], ksb),
        (vs.at[0], vsb),
        (km.at[0], kmb),
        (vm.at[0], vmb),
        (ck.at[0], c_ref.at[pl.ds(0, kv_heads)]),
        (cv.at[0], c_ref.at[pl.ds(kv_heads, kv_heads)]),
    ]
    done = 0
    for ref in q_refs:
        pairs.append((q.at[0, :, pl.ds(done, ref.shape[1])], ref))
        done += ref.shape[1]
    copies = [pltpu.make_async_copy(a, b, sem.at[i]) for i, (a, b) in enumerate(pairs)]
    for copy in copies:
        copy.start()
    for copy in copies[:5]:
        copy.wait()
    per = width // BLOCK
    pad = jnp.zeros((width - ksb.shape[0], rows), f32)
    for part, (mant, exponent) in enumerate(((kmb, ksb), (vmb, vsb))):
        scale = jnp.concatenate([jnp.exp2(exponent[...].astype(f32)), pad], axis=0).T
        for g in range(kv_heads):
            kv_ref[:, pl.ds((part * kv_heads + g) * width, width)] = decoded(mant[:, pl.ds(g * width, width)], scale, g * per)
    kv_ref[:, pl.ds(2 * kv_heads * width, qsb.shape[1])] = qsb[...].astype(f32).astype(bf16)
    for copy in copies[5:]:
        copy.wait()


def bias_kernel(limit_ref, bias_ref, *, pieces, held, rows, source):
    width = bias_ref.shape[1]
    here = lax.axis_index("seq")
    limit = limit_ref[pl.ds(0, 1), :]
    done = 0
    for cached, d in pieces:
        size = held if cached else rows
        key = lax.broadcasted_iota(jnp.int32, (size, width), 0)
        token = lax.broadcasted_iota(jnp.int32, (size, width), 1)
        if cached:
            seen = source(here, d) * held + key < limit
        else:
            seen = source(here, d) * rows + key <= here * rows + token
        bias_ref[pl.ds(done, size), :] = jnp.where(seen, 0.0, NEG).astype(bf16)
        done += size


def attend_kernel(*refs, cs, bs, pick, kv_heads, width, group, first):
    q_ref, sc_ref, bias_ref = refs[:3]
    c_refs = refs[3 : 3 + cs]
    b_refs = refs[3 + cs : 3 + cs + bs]
    out_ref, k_all, v_all, staged, sem = refs[-5:]
    rows = q_ref.shape[0]
    held = c_refs[0].shape[-2]
    heads = q_ref.shape[1] // width
    per_kv = out_ref.shape[2] // width // kv_heads
    factor = math.log2(math.e) / math.sqrt(width)
    c_keys, c_values, blocks_kv = pick(c_refs, b_refs)
    count = len(c_keys)
    lowest = first // per_kv
    for n in range(k_all.shape[0]):
        g = lowest + n
        for d in range(count):
            k_all[n, pl.ds(d * held, held), pl.ds(0, width)] = c_keys[d](g)
            v_all[n, pl.ds(d * held, held), :] = c_values[d](g)
            at = pl.ds(count * held + d * rows, rows)
            k_all[n, at, pl.ds(0, width)] = blocks_kv[d][:, pl.ds(g * width, width)]
            v_all[n, at, :] = blocks_kv[d][:, pl.ds((kv_heads + g) * width, width)]
        k_all[n, :, pl.ds(width, width)] = bias_ref[...]
    mark = jnp.where(
        lax.broadcasted_iota(jnp.int32, (rows, width), 0) == lax.broadcasted_iota(jnp.int32, (rows, width), 1),
        1.0,
        0.0,
    ).astype(bf16)
    scale = jnp.exp2(sc_ref[...].astype(f32))
    per = width // BLOCK
    copies = []

    def scores(step):
        g = (first + step * group) // per_kv - lowest
        blocks = []
        for k in range(group):
            head = step * group + k
            value = decoded(q_ref[:, pl.ds(head * width, width)], scale, (first + head) * per)
            blocks.append(jnp.concatenate([value, mark], axis=1))
        return lax.dot_general(jnp.concatenate(blocks, axis=0), k_all[g], (((1,), (1,)), ((), ())), preferred_element_type=f32)

    steps = heads // group
    s = scores(0)
    for step in range(steps):
        g = (first + step * group) // per_kv - lowest
        later = scores(step + 1) if step + 1 < steps else None
        top = jnp.max(s, axis=1, keepdims=True)
        w = jnp.exp2((s - top) * factor)
        total = jnp.sum(w, axis=1, keepdims=True)
        o = jnp.dot(w.astype(bf16), v_all[g], preferred_element_type=f32)
        o = (o / total).astype(bf16)
        s = later
        for k in range(group):
            staged[:, pl.ds((step * group + k) * width, width)] = o[k * rows : (k + 1) * rows]
        cols = pl.ds(step * group * width, group * width)
        to = pl.ds((first + step * group) * width, group * width)
        copy = pltpu.make_async_copy(staged.at[:, cols], out_ref.at[0, :, to], sem.at[step])
        copy.start()
        copies.append(copy)
    for copy in copies:
        copy.wait()


def blocks_of(q_ref, group, step, width, mark):
    return jnp.concatenate(
        [jnp.concatenate([q_ref[:, pl.ds((step * group + k) * width, width)], mark], axis=1) for k in range(group)], axis=0
    )


def token_marks(rows, width):
    shape = (rows, width)
    return jnp.where(lax.broadcasted_iota(jnp.int32, shape, 0) == lax.broadcasted_iota(jnp.int32, shape, 1), 1.0, 0.0).astype(bf16)


def product(q, k):
    return lax.dot_general(q, k, (((1,), (1,)), ((), ())), preferred_element_type=f32)


def send(staged, out_ref, sem, step, group, width, first, o):
    rows = staged.shape[0]
    for k in range(group):
        staged[:, pl.ds((step * group + k) * width, width)] = o[k * rows : (k + 1) * rows]
    here = pl.ds(step * group * width, group * width)
    there = pl.ds((first + step * group) * width, group * width)
    return pltpu.make_async_copy(staged.at[:, here], out_ref.at[0, :, there], sem.at[step])


def gather(k_all, v_all, c_refs, b_refs, bias_ref, lowest, first, kv_heads):
    width = v_all.shape[2]
    for n in range(k_all.shape[0]):
        g = lowest + n
        done = 0
        for ref in c_refs:
            at = pl.ds(done, ref.shape[1])
            k_all[n, at, pl.ds(0, width)] = ref[g]
            v_all[n, at, :] = ref[kv_heads + g]
            done += ref.shape[1]
        for ref in b_refs:
            at = pl.ds(done, ref.shape[0])
            k_all[n, at, pl.ds(0, width)] = ref[:, pl.ds(g * width, width)]
            v_all[n, at, :] = ref[:, pl.ds((kv_heads + g) * width, width)]
            done += ref.shape[0]
        k_all[n, :, pl.ds(width, width)] = bias_ref[pl.ds(first, done), :]


def early_kernel(*refs, cs, bs, heads, kv_heads, width, group, first):
    q_ref, sc_ref, bias_ref = refs[:3]
    c_refs, b_refs = refs[3 : 3 + cs], refs[3 + cs : 3 + cs + bs]
    qd, acc, top_ref, total_ref, k_all, v_all = refs[3 + cs + bs :]
    rows = q_ref.shape[0]
    here = q_ref.shape[1] // width
    per_kv = heads // kv_heads
    factor = math.log2(math.e) / math.sqrt(width)
    lowest = first // per_kv
    gather(k_all, v_all, c_refs, b_refs, bias_ref, lowest, 0, kv_heads)
    mark = token_marks(rows, width)
    scale = jnp.exp2(sc_ref[...].astype(f32))
    for head in range(here):
        cols = pl.ds(head * width, width)
        qd[:, cols] = decoded(q_ref[:, cols], scale, (first + head) * (width // BLOCK))
    steps = here // group
    s = product(blocks_of(qd, group, 0, width, mark), k_all[0])
    for step in range(steps):
        g = (first + step * group) // per_kv - lowest
        later = None
        if step + 1 < steps:
            later = product(blocks_of(qd, group, step + 1, width, mark), k_all[(first + (step + 1) * group) // per_kv - lowest])
        top = jnp.max(s, axis=1, keepdims=True)
        w = jnp.exp2((s - top) * factor)
        total = jnp.sum(w, axis=1, keepdims=True)
        at = pl.ds(step * group * rows, group * rows)
        acc[at, :] = jnp.dot(w.astype(bf16), v_all[g], preferred_element_type=f32)
        top_ref[at, :] = jnp.broadcast_to(top, (group * rows, width))
        total_ref[at, :] = jnp.broadcast_to(total, (group * rows, width))
        s = later


def late_kernel(*refs, cs, bs, parts, kv_heads, width, group):
    bias_ref = refs[0]
    c_refs, b_refs = refs[1 : 1 + cs], refs[1 + cs : 1 + cs + bs]
    states = [refs[1 + cs + bs + 4 * n : 5 + cs + bs + 4 * n] for n in range(parts)]
    out_ref, k_all, v_all, staged, sem = refs[-5:]
    rows = staged.shape[0]
    per_kv = out_ref.shape[2] // width // kv_heads
    factor = math.log2(math.e) / math.sqrt(width)
    keys = k_all.shape[1]
    gather(k_all, v_all, c_refs, b_refs, bias_ref, 0, bias_ref.shape[0] - keys, kv_heads)
    mark = token_marks(rows, width)
    todo = []
    for state in states:
        for step in range(state[0].shape[1] // width // group):
            todo.append((state, step, len(todo) * group // per_kv))
    state, step, g = todo[0]
    s = product(blocks_of(state[0], group, step, width, mark), k_all[g])
    copies = []
    for n, (state, step, g) in enumerate(todo):
        later = None
        if n + 1 < len(todo):
            later = product(blocks_of(todo[n + 1][0][0], group, todo[n + 1][1], width, mark), k_all[todo[n + 1][2]])
        _, acc, top_ref, total_ref = state
        at = pl.ds(step * group * rows, group * rows)
        old = top_ref[at, :]
        top = jnp.maximum(old, jnp.broadcast_to(jnp.max(s, axis=1, keepdims=True), old.shape))
        keep = jnp.exp2((old - top) * factor)
        w = jnp.exp2((s - jnp.concatenate([top] * pl.cdiv(keys, width), axis=1)[:, :keys]) * factor)
        total = total_ref[at, :] * keep + jnp.sum(w, axis=1, keepdims=True)
        o = acc[at, :] * keep + jnp.dot(w.astype(bf16), v_all[g], preferred_element_type=f32)
        copies.append(send(staged, out_ref, sem, n, group, width, 0, (o / total).astype(bf16)))
        copies[-1].start()
        s = later
    for copy in copies:
        copy.wait()


def in_hbm(x):
    return pltpu.with_memory_space_constraint(x, pltpu.MemorySpace.HBM)


def natural(here, d):
    return jnp.int32(d)


def mirrored(here, d):
    return lax.bitwise_xor(here, d)


NEAR = [(0, 1), (1, 0), (2, 3), (3, 2)]
FAR = [(0, 2), (2, 0), (1, 3), (3, 1)]


def pick_natural(c_refs, b_refs):
    c, b = c_refs[0], b_refs[0]
    count = c.shape[0]
    kv_heads = c.shape[1] // 2
    keys = [lambda g, d=d: c[d, g] for d in range(count)]
    values = [lambda g, d=d: c[d, kv_heads + g] for d in range(count)]
    return keys, values, [b.at[d] for d in range(count)]


def pick_mirrored(c_refs, b_refs):
    kv_heads = c_refs[0].shape[0] // 2
    keys = [lambda g, c=c: c[g] for c in c_refs]
    values = [lambda g, c=c: c[kv_heads + g] for c in c_refs]
    return keys, values, b_refs


def body(q_mant, q_scale, key_m, key_e, value_m, value_e, cached_k, cached_v, start):
    _, rows, features = q_mant.shape
    _, kv_heads, held, width = cached_k.shape
    count = lax.axis_size("seq")
    sections = lax.axis_size("section")
    heads = features // width
    keys = count * (held + rows)
    mirror = count == len(NEAR)
    slots = range(count)
    if mirror:
        early, late = slots[:-1], slots[-1:]
    else:
        early, late = slots, ()
    pieces = [(cached, d) for part in (early, late) for cached in (True, False) for d in part]
    sizes = [heads * n // sum(SHARES) for n in SHARES]
    kv, cached, *q = pl.pallas_call(
        functools.partial(first_kernel, width=width),
        out_shape=(
            jax.ShapeDtypeStruct((rows, 2 * kv_heads * width + q_scale.shape[2]), bf16),
            jax.ShapeDtypeStruct((2 * kv_heads, held, width), bf16),
            *(jax.ShapeDtypeStruct((rows, n * width), bf16) for n in sizes),
        ),
        in_specs=[HBM] * 8,
        out_specs=(VMEM,) * (2 + len(sizes)),
        scratch_shapes=[
            pltpu.VMEM(q_scale.shape[1:], jnp.int32),
            pltpu.VMEM(key_m.shape[1:], bf16),
            pltpu.VMEM((key_e.shape[2], rows), jnp.int32),
            pltpu.VMEM(value_m.shape[1:], bf16),
            pltpu.VMEM((value_e.shape[2], rows), jnp.int32),
            pltpu.SemaphoreType.DMA((7 + len(sizes),)),
        ],
        compiler_params=pltpu.CompilerParams(vmem_limit_bytes=8 << 20),
        name="first",
    )(*(
        in_hbm(x)
        for x in (q_mant, q_scale, key_m, jnp.swapaxes(key_e, 1, 2), value_m, jnp.swapaxes(value_e, 1, 2), cached_k, cached_v)
    ))
    limits = jnp.broadcast_to(start.reshape(1, 1), (8, width))
    bias = pl.pallas_call(
        functools.partial(bias_kernel, pieces=pieces, held=held, rows=rows, source=mirrored if mirror else natural),
        out_shape=jax.ShapeDtypeStruct((keys, width), bf16),
        in_specs=[VMEM],
        out_specs=VMEM,
        compiler_params=pltpu.CompilerParams(vmem_limit_bytes=8 << 20),
        name="bias",
    )(limits)
    relay = [(i, (i + 1) % sections) for i in range(sections)]
    kv = lax.ppermute(kv, "section", relay)
    kv, scale = kv[:, : 2 * kv_heads * width], kv[:, 2 * kv_heads * width :]
    q = [lax.ppermute(x, "section", relay) for x in q]
    if mirror:
        near = lax.ppermute(cached, "seq", NEAR)
        far = lax.ppermute(cached, "seq", FAR)
        c = [cached, near, far, lax.ppermute(far, "seq", NEAR)]
        far = lax.ppermute(kv, "seq", FAR)
        near = lax.ppermute(kv, "seq", NEAR)
        b = [kv, near, far, lax.ppermute(far, "seq", NEAR)]
    else:
        c = [lax.all_gather(cached, "seq", axis=0)]
        b = [lax.all_gather(kv, "seq", axis=0)]
    group = 4
    limit = (8 << 20) + keys * width * kv_heads * 8 + keys * group * rows * 12 + 4 * rows * features
    if mirror:
        first, states = 0, []
        most = len(early) * (held + rows)
        for x, n in zip(q, sizes):
            held_heads = max(1, n * kv_heads // heads)
            call = pl.pallas_call(
                functools.partial(
                    early_kernel, cs=len(early), bs=len(early), heads=heads, kv_heads=kv_heads, width=width, group=group, first=first
                ),
                out_shape=(jax.ShapeDtypeStruct((rows, n * width), bf16),) + (jax.ShapeDtypeStruct((n * rows, width), f32),) * 3,
                in_specs=[VMEM] * (3 + 2 * len(early)),
                out_specs=(VMEM,) * 4,
                scratch_shapes=[pltpu.VMEM((held_heads, most, 2 * width), bf16), pltpu.VMEM((held_heads, most, width), bf16)],
                compiler_params=pltpu.CompilerParams(vmem_limit_bytes=limit),
                name="early",
            )
            states += call(x, scale, bias, *c[: len(early)], *b[: len(early)])
            first += n
        return pl.pallas_call(
            functools.partial(
                late_kernel, cs=len(late), bs=len(late), parts=len(sizes), kv_heads=kv_heads, width=width, group=group
            ),
            out_shape=jax.ShapeDtypeStruct((1, rows, features), bf16),
            in_specs=[VMEM] * (1 + 2 * len(late) + len(states)),
            out_specs=pl.BlockSpec(memory_space=pl.ANY),
            scratch_shapes=[
                pltpu.VMEM((kv_heads, keys - most, 2 * width), bf16),
                pltpu.VMEM((kv_heads, keys - most, width), bf16),
                pltpu.VMEM((rows, features), bf16),
                pltpu.SemaphoreType.DMA((heads // group,)),
            ],
            compiler_params=pltpu.CompilerParams(vmem_limit_bytes=limit),
            name="late",
        )(bias, *c[len(early) :], *b[len(early) :], *states)
    out, first = (), 0
    for x, n in zip(q, sizes):
        held_heads = max(1, n * kv_heads // heads)
        out = (
            pl.pallas_call(
                functools.partial(
                    attend_kernel,
                    cs=len(c),
                    bs=len(b),
                    pick=pick_mirrored if mirror else pick_natural,
                    kv_heads=kv_heads,
                    width=width,
                    group=group,
                    first=first,
                ),
                out_shape=jax.ShapeDtypeStruct((1, rows, features), bf16),
                in_specs=[VMEM] * (3 + len(c) + len(b)) + [pl.BlockSpec(memory_space=pl.ANY)] * len(out),
                out_specs=pl.BlockSpec(memory_space=pl.ANY),
                scratch_shapes=[
                    pltpu.VMEM((held_heads, keys, 2 * width), bf16),
                    pltpu.VMEM((held_heads, keys, width), bf16),
                    pltpu.VMEM((rows, n * width), bf16),
                    pltpu.SemaphoreType.DMA((n // group,)),
                ],
                input_output_aliases={3 + len(c) + len(b): 0} if out else {},
                compiler_params=pltpu.CompilerParams(vmem_limit_bytes=limit),
            )(x, scale, bias, *c, *b, *out),
        )
        first += n
    return out[0]


SHARES = (1, 1)


def solution(mesh):
    rows = P("section", "seq", "tensor")

    step = jax.shard_map(
        body,
        mesh=mesh,
        in_specs=(rows,) * 6 + (P("section", "tensor", "seq", None),) * 2 + (P("section"),),
        out_specs=rows,
        check_vma=False,
    )
    if mesh.shape["seq"] != len(NEAR):
        return step
    return step
```

```python
import functools
import math

import jax
import jax.numpy as jnp
from jax import lax
from jax.experimental import pallas as pl
from jax.experimental.pallas import tpu as pltpu
from jax.sharding import PartitionSpec as P


NEG = -1e30
VMEM = pl.BlockSpec(memory_space=pltpu.MemorySpace.VMEM)
HBM = pl.BlockSpec(memory_space=pltpu.MemorySpace.HBM)
BLOCK = 32
bf16, f32 = jnp.bfloat16, jnp.float32


def spread(scale, first):
    lanes = lax.broadcasted_iota(jnp.int32, scale.shape, 1)
    return jnp.take_along_axis(scale, first + lanes // BLOCK, axis=1)


def decoded(mantissa, scale, first):
    return (mantissa.astype(f32) * spread(scale, first)).astype(bf16)


def first_kernel(*refs, width):
    q, qs, km, ks, vm, vs, ck, cv, kv_ref, c_ref = refs[:10]
    q_refs = refs[10:-6]
    qsb, kmb, ksb, vmb, vsb, sem = refs[-6:]
    _, kv_heads, _, _ = ck.shape
    rows = kv_ref.shape[0]
    pairs = [
        (qs.at[0], qsb),
        (ks.at[0], ksb),
        (vs.at[0], vsb),
        (km.at[0], kmb),
        (vm.at[0], vmb),
        (ck.at[0], c_ref.at[pl.ds(0, kv_heads)]),
        (cv.at[0], c_ref.at[pl.ds(kv_heads, kv_heads)]),
    ]
    done = 0
    for ref in q_refs:
        pairs.append((q.at[0, :, pl.ds(done, ref.shape[1])], ref))
        done += ref.shape[1]
    copies = [pltpu.make_async_copy(a, b, sem.at[i]) for i, (a, b) in enumerate(pairs)]
    for copy in copies:
        copy.start()
    for copy in copies[:5]:
        copy.wait()
    per = width // BLOCK
    pad = jnp.zeros((width - ksb.shape[0], rows), f32)
    for part, (mant, exponent) in enumerate(((kmb, ksb), (vmb, vsb))):
        scale = jnp.concatenate([jnp.exp2(exponent[...].astype(f32)), pad], axis=0).T
        for g in range(kv_heads):
            kv_ref[:, pl.ds((part * kv_heads + g) * width, width)] = decoded(mant[:, pl.ds(g * width, width)], scale, g * per)
    kv_ref[:, pl.ds(2 * kv_heads * width, qsb.shape[1])] = qsb[...].astype(f32).astype(bf16)
    for copy in copies[5:]:
        copy.wait()


def bias_kernel(limit_ref, bias_ref, *, pieces, held, rows, source):
    width = bias_ref.shape[1]
    here = lax.axis_index("seq")
    limit = limit_ref[pl.ds(0, 1), :]
    done = 0
    for cached, d in pieces:
        size = held if cached else rows
        key = lax.broadcasted_iota(jnp.int32, (size, width), 0)
        token = lax.broadcasted_iota(jnp.int32, (size, width), 1)
        if cached:
            seen = source(here, d) * held + key < limit
        else:
            seen = source(here, d) * rows + key <= here * rows + token
        bias_ref[pl.ds(done, size), :] = jnp.where(seen, 0.0, NEG).astype(bf16)
        done += size


def attend_kernel(*refs, cs, bs, pick, kv_heads, width, group, first):
    q_ref, sc_ref, bias_ref = refs[:3]
    c_refs = refs[3 : 3 + cs]
    b_refs = refs[3 + cs : 3 + cs + bs]
    out_ref, k_all, v_all, staged, sem = refs[-5:]
    rows = q_ref.shape[0]
    held = c_refs[0].shape[-2]
    heads = q_ref.shape[1] // width
    per_kv = out_ref.shape[2] // width // kv_heads
    factor = math.log2(math.e) / math.sqrt(width)
    c_keys, c_values, blocks_kv = pick(c_refs, b_refs)
    count = len(c_keys)
    lowest = first // per_kv
    for n in range(k_all.shape[0]):
        g = lowest + n
        for d in range(count):
            k_all[n, pl.ds(d * held, held), pl.ds(0, width)] = c_keys[d](g)
            v_all[n, pl.ds(d * held, held), :] = c_values[d](g)
            at = pl.ds(count * held + d * rows, rows)
            k_all[n, at, pl.ds(0, width)] = blocks_kv[d][:, pl.ds(g * width, width)]
            v_all[n, at, :] = blocks_kv[d][:, pl.ds((kv_heads + g) * width, width)]
        k_all[n, :, pl.ds(width, width)] = bias_ref[...]
    mark = jnp.where(
        lax.broadcasted_iota(jnp.int32, (rows, width), 0) == lax.broadcasted_iota(jnp.int32, (rows, width), 1),
        1.0,
        0.0,
    ).astype(bf16)
    scale = jnp.exp2(sc_ref[...].astype(f32))
    per = width // BLOCK
    copies = []

    def scores(step):
        g = (first + step * group) // per_kv - lowest
        blocks = []
        for k in range(group):
            head = step * group + k
            value = decoded(q_ref[:, pl.ds(head * width, width)], scale, (first + head) * per)
            blocks.append(jnp.concatenate([value, mark], axis=1))
        return lax.dot_general(jnp.concatenate(blocks, axis=0), k_all[g], (((1,), (1,)), ((), ())), preferred_element_type=f32)

    steps = heads // group
    s = scores(0)
    for step in range(steps):
        g = (first + step * group) // per_kv - lowest
        later = scores(step + 1) if step + 1 < steps else None
        top = jnp.max(s, axis=1, keepdims=True)
        w = jnp.exp2((s - top) * factor)
        total = jnp.sum(w, axis=1, keepdims=True)
        o = jnp.dot(w.astype(bf16), v_all[g], preferred_element_type=f32)
        o = (o / total).astype(bf16)
        s = later
        for k in range(group):
            staged[:, pl.ds((step * group + k) * width, width)] = o[k * rows : (k + 1) * rows]
        cols = pl.ds(step * group * width, group * width)
        to = pl.ds((first + step * group) * width, group * width)
        copy = pltpu.make_async_copy(staged.at[:, cols], out_ref.at[0, :, to], sem.at[step])
        copy.start()
        copies.append(copy)
    for copy in copies:
        copy.wait()


def blocks_of(q_ref, group, step, width, mark):
    return jnp.concatenate(
        [jnp.concatenate([q_ref[:, pl.ds((step * group + k) * width, width)], mark], axis=1) for k in range(group)], axis=0
    )


def token_marks(rows, width):
    shape = (rows, width)
    return jnp.where(lax.broadcasted_iota(jnp.int32, shape, 0) == lax.broadcasted_iota(jnp.int32, shape, 1), 1.0, 0.0).astype(bf16)


def product(q, k):
    return lax.dot_general(q, k, (((1,), (1,)), ((), ())), preferred_element_type=f32)


def send(staged, out_ref, sem, step, group, width, first, o):
    rows = staged.shape[0]
    for k in range(group):
        staged[:, pl.ds((step * group + k) * width, width)] = o[k * rows : (k + 1) * rows]
    here = pl.ds(step * group * width, group * width)
    there = pl.ds((first + step * group) * width, group * width)
    return pltpu.make_async_copy(staged.at[:, here], out_ref.at[0, :, there], sem.at[step])


def gather(k_all, v_all, c_refs, b_refs, bias_ref, lowest, first, kv_heads):
    width = v_all.shape[2]
    for n in range(k_all.shape[0]):
        g = lowest + n
        done = 0
        for ref in c_refs:
            at = pl.ds(done, ref.shape[1])
            k_all[n, at, pl.ds(0, width)] = ref[g]
            v_all[n, at, :] = ref[kv_heads + g]
            done += ref.shape[1]
        for ref in b_refs:
            at = pl.ds(done, ref.shape[0])
            k_all[n, at, pl.ds(0, width)] = ref[:, pl.ds(g * width, width)]
            v_all[n, at, :] = ref[:, pl.ds((kv_heads + g) * width, width)]
            done += ref.shape[0]
        k_all[n, pl.ds(0, done), pl.ds(width, width)] = bias_ref[pl.ds(first, done), :]
        if done < k_all.shape[1]:
            rest = pl.ds(done, k_all.shape[1] - done)
            k_all[n, rest, pl.ds(0, width)] = jnp.zeros((rest.size, width), bf16)
            k_all[n, rest, pl.ds(width, width)] = jnp.full((rest.size, width), NEG, bf16)
            v_all[n, rest, :] = jnp.zeros((rest.size, width), bf16)


def early_kernel(*refs, cs, bs, heads, kv_heads, width, group, first):
    q_ref, sc_ref, bias_ref = refs[:3]
    c_refs, b_refs = refs[3 : 3 + cs], refs[3 + cs : 3 + cs + bs]
    qd, acc, top_ref, total_ref, k_all, v_all = refs[3 + cs + bs :]
    rows = q_ref.shape[0]
    here = q_ref.shape[1] // width
    per_kv = heads // kv_heads
    factor = math.log2(math.e) / math.sqrt(width)
    lowest = first // per_kv
    gather(k_all, v_all, c_refs, b_refs, bias_ref, lowest, 0, kv_heads)
    mark = token_marks(rows, width)
    scale = jnp.exp2(sc_ref[...].astype(f32))
    for head in range(here):
        cols = pl.ds(head * width, width)
        qd[:, cols] = decoded(q_ref[:, cols], scale, (first + head) * (width // BLOCK))
    steps = here // group
    s = product(blocks_of(qd, group, 0, width, mark), k_all[0])
    for step in range(steps):
        g = (first + step * group) // per_kv - lowest
        later = None
        if step + 1 < steps:
            later = product(blocks_of(qd, group, step + 1, width, mark), k_all[(first + (step + 1) * group) // per_kv - lowest])
        top = jnp.max(s, axis=1, keepdims=True)
        w = jnp.exp2((s - top) * factor)
        total = jnp.sum(w, axis=1, keepdims=True)
        at = pl.ds(step * group * rows, group * rows)
        acc[at, :] = jnp.dot(w.astype(bf16), v_all[g], preferred_element_type=f32)
        top_ref[at, :] = jnp.broadcast_to(top, (group * rows, width))
        total_ref[at, :] = jnp.broadcast_to(total, (group * rows, width))
        s = later


def late_kernel(*refs, cs, bs, parts, kv_heads, width, group, lead, skip):
    first_tokens = lax.axis_index("seq") == 0
    pl.when(first_tokens if lead else jnp.logical_not(first_tokens))(
        functools.partial(finish, refs, cs, bs, parts, kv_heads, width, group, skip)
    )


def finish(refs, cs, bs, parts, kv_heads, width, group, skip):
    bias_ref = refs[0]
    c_refs, b_refs = refs[1 : 1 + cs], refs[1 + cs : 1 + cs + bs]
    states = [refs[1 + cs + bs + 4 * n : 5 + cs + bs + 4 * n] for n in range(parts)]
    out_ref, k_all, v_all, staged, sem = refs[-5:]
    rows = staged.shape[0]
    per_kv = out_ref.shape[2] // width // kv_heads
    factor = math.log2(math.e) / math.sqrt(width)
    keys = k_all.shape[1]
    gather(k_all, v_all, c_refs, b_refs, bias_ref, 0, skip, kv_heads)
    mark = token_marks(rows, width)
    todo = []
    for state in states:
        for step in range(state[0].shape[1] // width // group):
            todo.append((state, step, len(todo) * group // per_kv))
    state, step, g = todo[0]
    s = product(blocks_of(state[0], group, step, width, mark), k_all[g])
    copies = []
    for n, (state, step, g) in enumerate(todo):
        later = None
        if n + 1 < len(todo):
            later = product(blocks_of(todo[n + 1][0][0], group, todo[n + 1][1], width, mark), k_all[todo[n + 1][2]])
        _, acc, top_ref, total_ref = state
        at = pl.ds(step * group * rows, group * rows)
        old = top_ref[at, :]
        top = jnp.maximum(old, jnp.broadcast_to(jnp.max(s, axis=1, keepdims=True), old.shape))
        keep = jnp.exp2((old - top) * factor)
        w = jnp.exp2((s - jnp.concatenate([top] * pl.cdiv(keys, width), axis=1)[:, :keys]) * factor)
        total = total_ref[at, :] * keep + jnp.sum(w, axis=1, keepdims=True)
        o = acc[at, :] * keep + jnp.dot(w.astype(bf16), v_all[g], preferred_element_type=f32)
        copies.append(send(staged, out_ref, sem, n, group, width, 0, (o / total).astype(bf16)))
        copies[-1].start()
        s = later
    for copy in copies:
        copy.wait()


def in_hbm(x):
    return pltpu.with_memory_space_constraint(x, pltpu.MemorySpace.HBM)


def natural(here, d):
    return jnp.int32(d)


def mirrored(here, d):
    return lax.bitwise_xor(here, d)


NEAR = [(0, 1), (1, 0), (2, 3), (3, 2)]
FAR = [(0, 2), (2, 0), (1, 3), (3, 1)]


def pick_natural(c_refs, b_refs):
    c, b = c_refs[0], b_refs[0]
    count = c.shape[0]
    kv_heads = c.shape[1] // 2
    keys = [lambda g, d=d: c[d, g] for d in range(count)]
    values = [lambda g, d=d: c[d, kv_heads + g] for d in range(count)]
    return keys, values, [b.at[d] for d in range(count)]


def pick_mirrored(c_refs, b_refs):
    kv_heads = c_refs[0].shape[0] // 2
    keys = [lambda g, c=c: c[g] for c in c_refs]
    values = [lambda g, c=c: c[kv_heads + g] for c in c_refs]
    return keys, values, b_refs


def body(q_mant, q_scale, key_m, key_e, value_m, value_e, cached_k, cached_v, start):
    _, rows, features = q_mant.shape
    _, kv_heads, held, width = cached_k.shape
    count = lax.axis_size("seq")
    sections = lax.axis_size("section")
    heads = features // width
    keys = count * (held + rows)
    mirror = count == len(NEAR)
    slots = range(count)
    if mirror:
        early, late = slots[:-1], slots[-1:]
    else:
        early, late = slots, ()
    pieces = [(cached, d) for part in (early, late) for cached in (True, False) for d in part]
    sizes = [heads * n // sum(SHARES) for n in SHARES]
    kv, cached, *q = pl.pallas_call(
        functools.partial(first_kernel, width=width),
        out_shape=(
            jax.ShapeDtypeStruct((rows, 2 * kv_heads * width + q_scale.shape[2]), bf16),
            jax.ShapeDtypeStruct((2 * kv_heads, held, width), bf16),
            *(jax.ShapeDtypeStruct((rows, n * width), bf16) for n in sizes),
        ),
        in_specs=[HBM] * 8,
        out_specs=(VMEM,) * (2 + len(sizes)),
        scratch_shapes=[
            pltpu.VMEM(q_scale.shape[1:], jnp.int32),
            pltpu.VMEM(key_m.shape[1:], bf16),
            pltpu.VMEM((key_e.shape[2], rows), jnp.int32),
            pltpu.VMEM(value_m.shape[1:], bf16),
            pltpu.VMEM((value_e.shape[2], rows), jnp.int32),
            pltpu.SemaphoreType.DMA((7 + len(sizes),)),
        ],
        compiler_params=pltpu.CompilerParams(vmem_limit_bytes=8 << 20),
        name="first",
    )(*(
        in_hbm(x)
        for x in (q_mant, q_scale, key_m, jnp.swapaxes(key_e, 1, 2), value_m, jnp.swapaxes(value_e, 1, 2), cached_k, cached_v)
    ))
    limits = jnp.broadcast_to(start.reshape(1, 1), (8, width))
    bias = pl.pallas_call(
        functools.partial(bias_kernel, pieces=pieces, held=held, rows=rows, source=mirrored if mirror else natural),
        out_shape=jax.ShapeDtypeStruct((keys, width), bf16),
        in_specs=[VMEM],
        out_specs=VMEM,
        compiler_params=pltpu.CompilerParams(vmem_limit_bytes=8 << 20),
        name="bias",
    )(limits)
    relay = [(i, (i + 1) % sections) for i in range(sections)]
    kv = lax.ppermute(kv, "section", relay)
    kv, scale = kv[:, : 2 * kv_heads * width], kv[:, 2 * kv_heads * width :]
    q = [lax.ppermute(x, "section", relay) for x in q]
    if mirror:
        near = lax.ppermute(cached, "seq", NEAR)
        far = lax.ppermute(cached, "seq", FAR)
        c = [cached, near, far, lax.ppermute(far, "seq", NEAR)]
        far = lax.ppermute(kv, "seq", FAR)
        near = lax.ppermute(kv, "seq", NEAR)
        b = [kv, near, far, lax.ppermute(far, "seq", NEAR)]
    else:
        c = [lax.all_gather(cached, "seq", axis=0)]
        b = [lax.all_gather(kv, "seq", axis=0)]
    group = 4
    limit = (8 << 20) + keys * width * kv_heads * 8 + keys * group * rows * 12 + 4 * rows * features
    if mirror:
        first, states = 0, []
        most = len(early) * (held + rows)
        for x, n in zip(q, sizes):
            held_heads = max(1, n * kv_heads // heads)
            call = pl.pallas_call(
                functools.partial(
                    early_kernel, cs=len(early), bs=len(early), heads=heads, kv_heads=kv_heads, width=width, group=group, first=first
                ),
                out_shape=(jax.ShapeDtypeStruct((rows, n * width), bf16),) + (jax.ShapeDtypeStruct((n * rows, width), f32),) * 3,
                in_specs=[VMEM] * (3 + 2 * len(early)),
                out_specs=(VMEM,) * 4,
                scratch_shapes=[pltpu.VMEM((held_heads, most, 2 * width), bf16), pltpu.VMEM((held_heads, most, width), bf16)],
                compiler_params=pltpu.CompilerParams(vmem_limit_bytes=limit),
                name="early",
            )
            states += call(x, scale, bias, *c[: len(early)], *b[: len(early)])
            first += n
        out = []
        for lead in (True, False):
            blocks = [] if lead else b[len(early) :]
            fresh = len(late) * held + len(blocks) * rows
            padded = pl.cdiv(fresh, width) * width
            call = pl.pallas_call(
                functools.partial(
                    late_kernel,
                    cs=len(late),
                    bs=len(blocks),
                    parts=len(sizes),
                    kv_heads=kv_heads,
                    width=width,
                    group=2 * group,
                    lead=lead,
                    skip=most,
                ),
                out_shape=jax.ShapeDtypeStruct((1, rows, features), bf16),
                in_specs=[VMEM] * (1 + len(late) + len(blocks) + len(states)) + [pl.BlockSpec(memory_space=pl.ANY)] * len(out),
                out_specs=pl.BlockSpec(memory_space=pl.ANY),
                scratch_shapes=[
                    pltpu.VMEM((kv_heads, padded, 2 * width), bf16),
                    pltpu.VMEM((kv_heads, padded, width), bf16),
                    pltpu.VMEM((rows, features), bf16),
                    pltpu.SemaphoreType.DMA((heads // group,)),
                ],
                input_output_aliases={} if lead else {1 + len(late) + len(blocks) + len(states): 0},
                compiler_params=pltpu.CompilerParams(vmem_limit_bytes=limit),
                name="late",
            )
            out = [call(bias, *c[len(early) :], *blocks, *states, *out)]
        return out[0]
    out, first = (), 0
    for x, n in zip(q, sizes):
        held_heads = max(1, n * kv_heads // heads)
        out = (
            pl.pallas_call(
                functools.partial(
                    attend_kernel,
                    cs=len(c),
                    bs=len(b),
                    pick=pick_mirrored if mirror else pick_natural,
                    kv_heads=kv_heads,
                    width=width,
                    group=group,
                    first=first,
                ),
                out_shape=jax.ShapeDtypeStruct((1, rows, features), bf16),
                in_specs=[VMEM] * (3 + len(c) + len(b)) + [pl.BlockSpec(memory_space=pl.ANY)] * len(out),
                out_specs=pl.BlockSpec(memory_space=pl.ANY),
                scratch_shapes=[
                    pltpu.VMEM((held_heads, keys, 2 * width), bf16),
                    pltpu.VMEM((held_heads, keys, width), bf16),
                    pltpu.VMEM((rows, n * width), bf16),
                    pltpu.SemaphoreType.DMA((n // group,)),
                ],
                input_output_aliases={3 + len(c) + len(b): 0} if out else {},
                compiler_params=pltpu.CompilerParams(vmem_limit_bytes=limit),
            )(x, scale, bias, *c, *b, *out),
        )
        first += n
    return out[0]


SHARES = (1, 1)


def solution(mesh):
    rows = P("section", "seq", "tensor")

    step = jax.shard_map(
        body,
        mesh=mesh,
        in_specs=(rows,) * 6 + (P("section", "tensor", "seq", None),) * 2 + (P("section"),),
        out_specs=rows,
        check_vma=False,
    )
    if mesh.shape["seq"] != len(NEAR):
        return step
    return step
```

```python
import functools
import math

import jax
import jax.numpy as jnp
from jax import lax
from jax.experimental import pallas as pl
from jax.experimental.pallas import tpu as pltpu
from jax.sharding import PartitionSpec as P


NEG = -1e30
VMEM = pl.BlockSpec(memory_space=pltpu.MemorySpace.VMEM)
HBM = pl.BlockSpec(memory_space=pltpu.MemorySpace.HBM)
BLOCK = 32
bf16, f32 = jnp.bfloat16, jnp.float32


def spread(scale, first):
    lanes = lax.broadcasted_iota(jnp.int32, scale.shape, 1)
    return jnp.take_along_axis(scale, first + lanes // BLOCK, axis=1)


def decoded(mantissa, scale, first):
    return (mantissa.astype(f32) * spread(scale, first)).astype(bf16)


def first_kernel(*refs, width):
    q, qs, km, ks, vm, vs, ck, cv, kv_ref, c_ref = refs[:10]
    q_refs = refs[10:-6]
    qsb, kmb, ksb, vmb, vsb, sem = refs[-6:]
    _, kv_heads, _, _ = ck.shape
    rows = kv_ref.shape[0]
    pairs = [
        (qs.at[0], qsb),
        (ks.at[0], ksb),
        (vs.at[0], vsb),
        (km.at[0], kmb),
        (vm.at[0], vmb),
        (ck.at[0], c_ref.at[pl.ds(0, kv_heads)]),
        (cv.at[0], c_ref.at[pl.ds(kv_heads, kv_heads)]),
    ]
    done = 0
    for ref in q_refs:
        pairs.append((q.at[0, :, pl.ds(done, ref.shape[1])], ref))
        done += ref.shape[1]
    copies = [pltpu.make_async_copy(a, b, sem.at[i]) for i, (a, b) in enumerate(pairs)]
    for copy in copies:
        copy.start()
    for copy in copies[:5]:
        copy.wait()
    per = width // BLOCK
    pad = jnp.zeros((width - ksb.shape[0], rows), f32)
    for part, (mant, exponent) in enumerate(((kmb, ksb), (vmb, vsb))):
        scale = jnp.concatenate([jnp.exp2(exponent[...].astype(f32)), pad], axis=0).T
        for g in range(kv_heads):
            kv_ref[:, pl.ds((part * kv_heads + g) * width, width)] = decoded(mant[:, pl.ds(g * width, width)], scale, g * per)
    kv_ref[:, pl.ds(2 * kv_heads * width, qsb.shape[1])] = qsb[...].astype(f32).astype(bf16)
    for copy in copies[5:]:
        copy.wait()


def bias_kernel(limit_ref, bias_ref, *, pieces, held, rows, source):
    width = bias_ref.shape[1]
    here = lax.axis_index("seq")
    limit = limit_ref[pl.ds(0, 1), :]
    done = 0
    for cached, d in pieces:
        size = held if cached else rows
        key = lax.broadcasted_iota(jnp.int32, (size, width), 0)
        token = lax.broadcasted_iota(jnp.int32, (size, width), 1)
        if cached:
            seen = source(here, d) * held + key < limit
        else:
            seen = source(here, d) * rows + key <= here * rows + token
        bias_ref[pl.ds(done, size), :] = jnp.where(seen, 0.0, NEG).astype(bf16)
        done += size


def attend_kernel(*refs, cs, bs, pick, kv_heads, width, group, first):
    q_ref, sc_ref, bias_ref = refs[:3]
    c_refs = refs[3 : 3 + cs]
    b_refs = refs[3 + cs : 3 + cs + bs]
    out_ref, k_all, v_all, staged, sem = refs[-5:]
    rows = q_ref.shape[0]
    held = c_refs[0].shape[-2]
    heads = q_ref.shape[1] // width
    per_kv = out_ref.shape[2] // width // kv_heads
    factor = math.log2(math.e) / math.sqrt(width)
    c_keys, c_values, blocks_kv = pick(c_refs, b_refs)
    count = len(c_keys)
    lowest = first // per_kv
    for n in range(k_all.shape[0]):
        g = lowest + n
        for d in range(count):
            k_all[n, pl.ds(d * held, held), pl.ds(0, width)] = c_keys[d](g)
            v_all[n, pl.ds(d * held, held), :] = c_values[d](g)
            at = pl.ds(count * held + d * rows, rows)
            k_all[n, at, pl.ds(0, width)] = blocks_kv[d][:, pl.ds(g * width, width)]
            v_all[n, at, :] = blocks_kv[d][:, pl.ds((kv_heads + g) * width, width)]
        k_all[n, :, pl.ds(width, width)] = bias_ref[...]
    mark = jnp.where(
        lax.broadcasted_iota(jnp.int32, (rows, width), 0) == lax.broadcasted_iota(jnp.int32, (rows, width), 1),
        1.0,
        0.0,
    ).astype(bf16)
    scale = jnp.exp2(sc_ref[...].astype(f32))
    per = width // BLOCK
    copies = []

    def scores(step):
        g = (first + step * group) // per_kv - lowest
        blocks = []
        for k in range(group):
            head = step * group + k
            value = decoded(q_ref[:, pl.ds(head * width, width)], scale, (first + head) * per)
            blocks.append(jnp.concatenate([value, mark], axis=1))
        return lax.dot_general(jnp.concatenate(blocks, axis=0), k_all[g], (((1,), (1,)), ((), ())), preferred_element_type=f32)

    steps = heads // group
    s = scores(0)
    for step in range(steps):
        g = (first + step * group) // per_kv - lowest
        later = scores(step + 1) if step + 1 < steps else None
        top = jnp.max(s, axis=1, keepdims=True)
        w = jnp.exp2((s - top) * factor)
        total = jnp.sum(w, axis=1, keepdims=True)
        o = jnp.dot(w.astype(bf16), v_all[g], preferred_element_type=f32)
        o = (o / total).astype(bf16)
        s = later
        for k in range(group):
            staged[:, pl.ds((step * group + k) * width, width)] = o[k * rows : (k + 1) * rows]
        cols = pl.ds(step * group * width, group * width)
        to = pl.ds((first + step * group) * width, group * width)
        copy = pltpu.make_async_copy(staged.at[:, cols], out_ref.at[0, :, to], sem.at[step])
        copy.start()
        copies.append(copy)
    for copy in copies:
        copy.wait()


def blocks_of(q_ref, group, step, width, mark):
    return jnp.concatenate(
        [jnp.concatenate([q_ref[:, pl.ds((step * group + k) * width, width)], mark], axis=1) for k in range(group)], axis=0
    )


def token_marks(rows, width):
    shape = (rows, width)
    return jnp.where(lax.broadcasted_iota(jnp.int32, shape, 0) == lax.broadcasted_iota(jnp.int32, shape, 1), 1.0, 0.0).astype(bf16)


def product(q, k):
    return lax.dot_general(q, k, (((1,), (1,)), ((), ())), preferred_element_type=f32)


def send(staged, out_ref, sem, step, group, width, first, o):
    rows = staged.shape[0]
    for k in range(group):
        staged[:, pl.ds((step * group + k) * width, width)] = o[k * rows : (k + 1) * rows]
    here = pl.ds(step * group * width, group * width)
    there = pl.ds((first + step * group) * width, group * width)
    return pltpu.make_async_copy(staged.at[:, here], out_ref.at[0, :, there], sem.at[step])


def gather(k_all, v_all, c_refs, b_refs, bias_ref, lowest, first, kv_heads):
    width = v_all.shape[2]
    for n in range(k_all.shape[0]):
        g = lowest + n
        done = 0
        for ref in c_refs:
            at = pl.ds(done, ref.shape[1])
            k_all[n, at, pl.ds(0, width)] = ref[g]
            v_all[n, at, :] = ref[kv_heads + g]
            done += ref.shape[1]
        for ref in b_refs:
            at = pl.ds(done, ref.shape[0])
            k_all[n, at, pl.ds(0, width)] = ref[:, pl.ds(g * width, width)]
            v_all[n, at, :] = ref[:, pl.ds((kv_heads + g) * width, width)]
            done += ref.shape[0]
        k_all[n, pl.ds(0, done), pl.ds(width, width)] = bias_ref[pl.ds(first, done), :]
        if done < k_all.shape[1]:
            rest = pl.ds(done, k_all.shape[1] - done)
            k_all[n, rest, pl.ds(0, width)] = jnp.zeros((rest.size, width), bf16)
            k_all[n, rest, pl.ds(width, width)] = jnp.full((rest.size, width), NEG, bf16)
            v_all[n, rest, :] = jnp.zeros((rest.size, width), bf16)


def early_kernel(*refs, cs, bs, heads, kv_heads, width, group, first):
    q_ref, sc_ref, bias_ref = refs[:3]
    c_refs, b_refs = refs[3 : 3 + cs], refs[3 + cs : 3 + cs + bs]
    qd, acc, top_ref, total_ref, k_all, v_all = refs[3 + cs + bs :]
    rows = q_ref.shape[0]
    here = q_ref.shape[1] // width
    per_kv = heads // kv_heads
    factor = math.log2(math.e) / math.sqrt(width)
    lowest = first // per_kv
    gather(k_all, v_all, c_refs, b_refs, bias_ref, lowest, 0, kv_heads)
    mark = token_marks(rows, width)
    scale = jnp.exp2(sc_ref[...].astype(f32))
    for head in range(here):
        cols = pl.ds(head * width, width)
        qd[:, cols] = decoded(q_ref[:, cols], scale, (first + head) * (width // BLOCK))
    steps = here // group
    s = product(blocks_of(qd, group, 0, width, mark), k_all[0])
    for step in range(steps):
        g = (first + step * group) // per_kv - lowest
        later = None
        if step + 1 < steps:
            later = product(blocks_of(qd, group, step + 1, width, mark), k_all[(first + (step + 1) * group) // per_kv - lowest])
        top = jnp.max(s, axis=1, keepdims=True)
        w = jnp.exp2((s - top) * factor)
        total = jnp.sum(w, axis=1, keepdims=True)
        at = pl.ds(step * group * rows, group * rows)
        acc[at, :] = jnp.dot(w.astype(bf16), v_all[g], preferred_element_type=f32)
        top_ref[at, :] = jnp.broadcast_to(top, (group * rows, width))
        total_ref[at, :] = jnp.broadcast_to(total, (group * rows, width))
        s = later


def late_kernel(*refs, cs, bs, parts, kv_heads, width, group, lead, skip):
    first_tokens = lax.axis_index("seq") == 0
    pl.when(first_tokens if lead else jnp.logical_not(first_tokens))(
        functools.partial(finish, refs, cs, bs, parts, kv_heads, width, group, skip)
    )


def finish(refs, cs, bs, parts, kv_heads, width, group, skip):
    bias_ref = refs[0]
    c_refs, b_refs = refs[1 : 1 + cs], refs[1 + cs : 1 + cs + bs]
    states = [refs[1 + cs + bs + 4 * n : 5 + cs + bs + 4 * n] for n in range(parts)]
    out_ref, k_all, v_all, staged, sem = refs[-5:]
    rows = staged.shape[0]
    per_kv = out_ref.shape[2] // width // kv_heads
    factor = math.log2(math.e) / math.sqrt(width)
    keys = k_all.shape[1]
    gather(k_all, v_all, c_refs, b_refs, bias_ref, 0, skip, kv_heads)
    mark = token_marks(rows, width)
    todo = []
    for state in states:
        for step in range(state[0].shape[1] // width // group):
            todo.append((state, step, len(todo) * group // per_kv))
    state, step, g = todo[0]
    s = product(blocks_of(state[0], group, step, width, mark), k_all[g])
    copies = []
    for n, (state, step, g) in enumerate(todo):
        later = None
        if n + 1 < len(todo):
            later = product(blocks_of(todo[n + 1][0][0], group, todo[n + 1][1], width, mark), k_all[todo[n + 1][2]])
        _, acc, top_ref, total_ref = state
        at = pl.ds(step * group * rows, group * rows)
        old = top_ref[at, :]
        top = jnp.maximum(old, jnp.broadcast_to(jnp.max(s, axis=1, keepdims=True), old.shape))
        keep = jnp.exp2((old - top) * factor)
        w = jnp.exp2((s - jnp.concatenate([top] * pl.cdiv(keys, width), axis=1)[:, :keys]) * factor)
        total = total_ref[at, :] * keep + jnp.sum(w, axis=1, keepdims=True)
        o = acc[at, :] * keep + jnp.dot(w.astype(bf16), v_all[g], preferred_element_type=f32)
        copies.append(send(staged, out_ref, sem, n, group, width, 0, (o / total).astype(bf16)))
        copies[-1].start()
        s = later
    for copy in copies:
        copy.wait()


def in_hbm(x):
    return pltpu.with_memory_space_constraint(x, pltpu.MemorySpace.HBM)


def natural(here, d):
    return jnp.int32(d)


def mirrored(here, d):
    return lax.bitwise_xor(here, d)


NEAR = [(0, 1), (1, 0), (2, 3), (3, 2)]
FAR = [(0, 2), (2, 0), (1, 3), (3, 1)]


def pick_natural(c_refs, b_refs):
    c, b = c_refs[0], b_refs[0]
    count = c.shape[0]
    kv_heads = c.shape[1] // 2
    keys = [lambda g, d=d: c[d, g] for d in range(count)]
    values = [lambda g, d=d: c[d, kv_heads + g] for d in range(count)]
    return keys, values, [b.at[d] for d in range(count)]


def pick_mirrored(c_refs, b_refs):
    kv_heads = c_refs[0].shape[0] // 2
    keys = [lambda g, c=c: c[g] for c in c_refs]
    values = [lambda g, c=c: c[kv_heads + g] for c in c_refs]
    return keys, values, b_refs


def body(q_mant, q_scale, key_m, key_e, value_m, value_e, cached_k, cached_v, start):
    _, rows, features = q_mant.shape
    _, kv_heads, held, width = cached_k.shape
    count = lax.axis_size("seq")
    sections = lax.axis_size("section")
    heads = features // width
    keys = count * (held + rows)
    mirror = count == len(NEAR)
    slots = range(count)
    if mirror:
        early, late = slots[:-1], slots[-1:]
    else:
        early, late = slots, ()
    pieces = [(cached, d) for part in (early, late) for cached in (True, False) for d in part]
    sizes = [heads * n // sum(SHARES) for n in SHARES]
    kv, cached, *q = pl.pallas_call(
        functools.partial(first_kernel, width=width),
        out_shape=(
            jax.ShapeDtypeStruct((rows, 2 * kv_heads * width + q_scale.shape[2]), bf16),
            jax.ShapeDtypeStruct((2 * kv_heads, held, width), bf16),
            *(jax.ShapeDtypeStruct((rows, n * width), bf16) for n in sizes),
        ),
        in_specs=[HBM] * 8,
        out_specs=(VMEM,) * (2 + len(sizes)),
        scratch_shapes=[
            pltpu.VMEM(q_scale.shape[1:], jnp.int32),
            pltpu.VMEM(key_m.shape[1:], bf16),
            pltpu.VMEM((key_e.shape[2], rows), jnp.int32),
            pltpu.VMEM(value_m.shape[1:], bf16),
            pltpu.VMEM((value_e.shape[2], rows), jnp.int32),
            pltpu.SemaphoreType.DMA((7 + len(sizes),)),
        ],
        compiler_params=pltpu.CompilerParams(vmem_limit_bytes=8 << 20),
        name="first",
    )(*(
        in_hbm(x)
        for x in (q_mant, q_scale, key_m, jnp.swapaxes(key_e, 1, 2), value_m, jnp.swapaxes(value_e, 1, 2), cached_k, cached_v)
    ))
    limits = jnp.broadcast_to(start.reshape(1, 1), (8, width))
    bias = pl.pallas_call(
        functools.partial(bias_kernel, pieces=pieces, held=held, rows=rows, source=mirrored if mirror else natural),
        out_shape=jax.ShapeDtypeStruct((keys, width), bf16),
        in_specs=[VMEM],
        out_specs=VMEM,
        compiler_params=pltpu.CompilerParams(vmem_limit_bytes=8 << 20),
        name="bias",
    )(limits)
    relay = [(i, (i + 1) % sections) for i in range(sections)]
    kv = lax.ppermute(kv, "section", relay)
    kv, scale = kv[:, : 2 * kv_heads * width], kv[:, 2 * kv_heads * width :]
    q = [lax.ppermute(x, "section", relay) for x in q]
    if mirror:
        near = lax.ppermute(cached, "seq", NEAR)
        far = lax.ppermute(cached, "seq", FAR)
        c = [cached, near, far, lax.ppermute(far, "seq", NEAR)]
        far = lax.ppermute(kv, "seq", FAR)
        near = lax.ppermute(kv, "seq", NEAR)
        b = [kv, near, far, lax.ppermute(far, "seq", NEAR)]
    else:
        c = [lax.all_gather(cached, "seq", axis=0)]
        b = [lax.all_gather(kv, "seq", axis=0)]
    group = 4
    limit = (8 << 20) + keys * width * kv_heads * 8 + keys * group * rows * 12 + 4 * rows * features
    if mirror:
        first, states = 0, []
        most = len(early) * (held + rows)
        whole = pl.cdiv(most, width) * width
        for x, n in zip(q, sizes):
            held_heads = max(1, n * kv_heads // heads)
            call = pl.pallas_call(
                functools.partial(
                    early_kernel, cs=len(early), bs=len(early), heads=heads, kv_heads=kv_heads, width=width, group=2 * group, first=first
                ),
                out_shape=(jax.ShapeDtypeStruct((rows, n * width), bf16),) + (jax.ShapeDtypeStruct((n * rows, width), f32),) * 3,
                in_specs=[VMEM] * (3 + 2 * len(early)),
                out_specs=(VMEM,) * 4,
                scratch_shapes=[pltpu.VMEM((held_heads, whole, 2 * width), bf16), pltpu.VMEM((held_heads, whole, width), bf16)],
                compiler_params=pltpu.CompilerParams(vmem_limit_bytes=limit),
                name="early",
            )
            states += call(x, scale, bias, *c[: len(early)], *b[: len(early)])
            first += n
        out = []
        for lead in (True, False):
            blocks = [] if lead else b[len(early) :]
            fresh = len(late) * held + len(blocks) * rows
            padded = pl.cdiv(fresh, width) * width
            call = pl.pallas_call(
                functools.partial(
                    late_kernel,
                    cs=len(late),
                    bs=len(blocks),
                    parts=len(sizes),
                    kv_heads=kv_heads,
                    width=width,
                    group=2 * group,
                    lead=lead,
                    skip=most,
                ),
                out_shape=jax.ShapeDtypeStruct((1, rows, features), bf16),
                in_specs=[VMEM] * (1 + len(late) + len(blocks) + len(states)) + [pl.BlockSpec(memory_space=pl.ANY)] * len(out),
                out_specs=pl.BlockSpec(memory_space=pl.ANY),
                scratch_shapes=[
                    pltpu.VMEM((kv_heads, padded, 2 * width), bf16),
                    pltpu.VMEM((kv_heads, padded, width), bf16),
                    pltpu.VMEM((rows, features), bf16),
                    pltpu.SemaphoreType.DMA((heads // group,)),
                ],
                input_output_aliases={} if lead else {1 + len(late) + len(blocks) + len(states): 0},
                compiler_params=pltpu.CompilerParams(vmem_limit_bytes=limit),
                name="late",
            )
            out = [call(bias, *c[len(early) :], *blocks, *states, *out)]
        return out[0]
    out, first = (), 0
    for x, n in zip(q, sizes):
        held_heads = max(1, n * kv_heads // heads)
        out = (
            pl.pallas_call(
                functools.partial(
                    attend_kernel,
                    cs=len(c),
                    bs=len(b),
                    pick=pick_mirrored if mirror else pick_natural,
                    kv_heads=kv_heads,
                    width=width,
                    group=group,
                    first=first,
                ),
                out_shape=jax.ShapeDtypeStruct((1, rows, features), bf16),
                in_specs=[VMEM] * (3 + len(c) + len(b)) + [pl.BlockSpec(memory_space=pl.ANY)] * len(out),
                out_specs=pl.BlockSpec(memory_space=pl.ANY),
                scratch_shapes=[
                    pltpu.VMEM((held_heads, keys, 2 * width), bf16),
                    pltpu.VMEM((held_heads, keys, width), bf16),
                    pltpu.VMEM((rows, n * width), bf16),
                    pltpu.SemaphoreType.DMA((n // group,)),
                ],
                input_output_aliases={3 + len(c) + len(b): 0} if out else {},
                compiler_params=pltpu.CompilerParams(vmem_limit_bytes=limit),
            )(x, scale, bias, *c, *b, *out),
        )
        first += n
    return out[0]


SHARES = (1, 1)


def solution(mesh):
    rows = P("section", "seq", "tensor")

    step = jax.shard_map(
        body,
        mesh=mesh,
        in_specs=(rows,) * 6 + (P("section", "tensor", "seq", None),) * 2 + (P("section"),),
        out_specs=rows,
        check_vma=False,
    )
    if mesh.shape["seq"] != len(NEAR):
        return step
    return step
```

```python
import functools
import math

import jax
import jax.numpy as jnp
from jax import lax
from jax.experimental import pallas as pl
from jax.experimental.pallas import tpu as pltpu
from jax.sharding import PartitionSpec as P


NEG = -1e30
VMEM = pl.BlockSpec(memory_space=pltpu.MemorySpace.VMEM)
HBM = pl.BlockSpec(memory_space=pltpu.MemorySpace.HBM)
BLOCK = 32
bf16, f32 = jnp.bfloat16, jnp.float32


def spread(scale, first):
    lanes = lax.broadcasted_iota(jnp.int32, scale.shape, 1)
    return jnp.take_along_axis(scale, first + lanes // BLOCK, axis=1)


def decoded(mantissa, scale, first):
    return (mantissa.astype(f32) * spread(scale, first)).astype(bf16)


def first_kernel(*refs, width):
    q, qs, km, ks, vm, vs, ck, cv, kv_ref, c_ref = refs[:10]
    q_refs = refs[10:-6]
    qsb, kmb, ksb, vmb, vsb, sem = refs[-6:]
    _, kv_heads, _, _ = ck.shape
    rows = kv_ref.shape[0]
    pairs = [
        (qs.at[0], qsb),
        (ks.at[0], ksb),
        (vs.at[0], vsb),
        (km.at[0], kmb),
        (vm.at[0], vmb),
        (ck.at[0], c_ref.at[pl.ds(0, kv_heads)]),
        (cv.at[0], c_ref.at[pl.ds(kv_heads, kv_heads)]),
    ]
    done = 0
    for ref in q_refs:
        pairs.append((q.at[0, :, pl.ds(done, ref.shape[1])], ref))
        done += ref.shape[1]
    copies = [pltpu.make_async_copy(a, b, sem.at[i]) for i, (a, b) in enumerate(pairs)]
    for copy in copies:
        copy.start()
    for copy in copies[:5]:
        copy.wait()
    per = width // BLOCK
    pad = jnp.zeros((width - ksb.shape[0], rows), f32)
    for part, (mant, exponent) in enumerate(((kmb, ksb), (vmb, vsb))):
        scale = jnp.concatenate([jnp.exp2(exponent[...].astype(f32)), pad], axis=0).T
        for g in range(kv_heads):
            kv_ref[:, pl.ds((part * kv_heads + g) * width, width)] = decoded(mant[:, pl.ds(g * width, width)], scale, g * per)
    kv_ref[:, pl.ds(2 * kv_heads * width, qsb.shape[1])] = qsb[...].astype(f32).astype(bf16)
    for copy in copies[5:]:
        copy.wait()


def bias_kernel(limit_ref, bias_ref, *, pieces, held, rows, source):
    width = bias_ref.shape[1]
    here = lax.axis_index("seq")
    limit = limit_ref[pl.ds(0, 1), :]
    done = 0
    for cached, d in pieces:
        size = held if cached else rows
        key = lax.broadcasted_iota(jnp.int32, (size, width), 0)
        token = lax.broadcasted_iota(jnp.int32, (size, width), 1)
        if cached:
            seen = source(here, d) * held + key < limit
        else:
            seen = source(here, d) * rows + key <= here * rows + token
        bias_ref[pl.ds(done, size), :] = jnp.where(seen, 0.0, NEG).astype(bf16)
        done += size


def attend_kernel(*refs, cs, bs, pick, kv_heads, width, group, first):
    q_ref, sc_ref, bias_ref = refs[:3]
    c_refs = refs[3 : 3 + cs]
    b_refs = refs[3 + cs : 3 + cs + bs]
    out_ref, k_all, v_all, staged, sem = refs[-5:]
    rows = q_ref.shape[0]
    held = c_refs[0].shape[-2]
    heads = q_ref.shape[1] // width
    per_kv = out_ref.shape[2] // width // kv_heads
    factor = math.log2(math.e) / math.sqrt(width)
    c_keys, c_values, blocks_kv = pick(c_refs, b_refs)
    count = len(c_keys)
    lowest = first // per_kv
    for n in range(k_all.shape[0]):
        g = lowest + n
        for d in range(count):
            k_all[n, pl.ds(d * held, held), pl.ds(0, width)] = c_keys[d](g)
            v_all[n, pl.ds(d * held, held), :] = c_values[d](g)
            at = pl.ds(count * held + d * rows, rows)
            k_all[n, at, pl.ds(0, width)] = blocks_kv[d][:, pl.ds(g * width, width)]
            v_all[n, at, :] = blocks_kv[d][:, pl.ds((kv_heads + g) * width, width)]
        k_all[n, :, pl.ds(width, width)] = bias_ref[...]
    mark = jnp.where(
        lax.broadcasted_iota(jnp.int32, (rows, width), 0) == lax.broadcasted_iota(jnp.int32, (rows, width), 1),
        1.0,
        0.0,
    ).astype(bf16)
    scale = jnp.exp2(sc_ref[...].astype(f32))
    per = width // BLOCK
    copies = []

    def scores(step):
        g = (first + step * group) // per_kv - lowest
        blocks = []
        for k in range(group):
            head = step * group + k
            value = decoded(q_ref[:, pl.ds(head * width, width)], scale, (first + head) * per)
            blocks.append(jnp.concatenate([value, mark], axis=1))
        return lax.dot_general(jnp.concatenate(blocks, axis=0), k_all[g], (((1,), (1,)), ((), ())), preferred_element_type=f32)

    steps = heads // group
    s = scores(0)
    for step in range(steps):
        g = (first + step * group) // per_kv - lowest
        later = scores(step + 1) if step + 1 < steps else None
        top = jnp.max(s, axis=1, keepdims=True)
        w = jnp.exp2((s - top) * factor)
        total = jnp.sum(w, axis=1, keepdims=True)
        o = jnp.dot(w.astype(bf16), v_all[g], preferred_element_type=f32)
        o = (o / total).astype(bf16)
        s = later
        for k in range(group):
            staged[:, pl.ds((step * group + k) * width, width)] = o[k * rows : (k + 1) * rows]
        cols = pl.ds(step * group * width, group * width)
        to = pl.ds((first + step * group) * width, group * width)
        copy = pltpu.make_async_copy(staged.at[:, cols], out_ref.at[0, :, to], sem.at[step])
        copy.start()
        copies.append(copy)
    for copy in copies:
        copy.wait()


def blocks_of(q_ref, group, step, width, mark):
    return jnp.concatenate(
        [jnp.concatenate([q_ref[:, pl.ds((step * group + k) * width, width)], mark], axis=1) for k in range(group)], axis=0
    )


def token_marks(rows, width):
    shape = (rows, width)
    return jnp.where(lax.broadcasted_iota(jnp.int32, shape, 0) == lax.broadcasted_iota(jnp.int32, shape, 1), 1.0, 0.0).astype(bf16)


def product(q, k):
    return lax.dot_general(q, k, (((1,), (1,)), ((), ())), preferred_element_type=f32)


def send(staged, out_ref, sem, step, group, width, first, o):
    rows = staged.shape[0]
    for k in range(group):
        staged[:, pl.ds((step * group + k) * width, width)] = o[k * rows : (k + 1) * rows]
    here = pl.ds(step * group * width, group * width)
    there = pl.ds((first + step * group) * width, group * width)
    return pltpu.make_async_copy(staged.at[:, here], out_ref.at[0, :, there], sem.at[step])


def gather(k_all, v_all, c_refs, b_refs, bias_ref, lowest, first, kv_heads):
    width = v_all.shape[2]
    for n in range(k_all.shape[0]):
        g = lowest + n
        done = 0
        for ref in c_refs:
            at = pl.ds(done, ref.shape[1])
            k_all[n, at, pl.ds(0, width)] = ref[g]
            v_all[n, at, :] = ref[kv_heads + g]
            done += ref.shape[1]
        for ref in b_refs:
            at = pl.ds(done, ref.shape[0])
            k_all[n, at, pl.ds(0, width)] = ref[:, pl.ds(g * width, width)]
            v_all[n, at, :] = ref[:, pl.ds((kv_heads + g) * width, width)]
            done += ref.shape[0]
        k_all[n, pl.ds(0, done), pl.ds(width, width)] = bias_ref[pl.ds(first, done), :]
        if done < k_all.shape[1]:
            rest = pl.ds(done, k_all.shape[1] - done)
            k_all[n, rest, pl.ds(0, width)] = jnp.zeros((rest.size, width), bf16)
            k_all[n, rest, pl.ds(width, width)] = jnp.full((rest.size, width), NEG, bf16)
            v_all[n, rest, :] = jnp.zeros((rest.size, width), bf16)


def early_kernel(*refs, cs, bs, heads, kv_heads, width, group, first):
    q_ref, sc_ref, bias_ref = refs[:3]
    c_refs, b_refs = refs[3 : 3 + cs], refs[3 + cs : 3 + cs + bs]
    qd, acc, top_ref, total_ref, k_all, v_all = refs[3 + cs + bs :]
    rows = q_ref.shape[0]
    here = q_ref.shape[1] // width
    per_kv = heads // kv_heads
    factor = math.log2(math.e) / math.sqrt(width)
    lowest = first // per_kv
    gather(k_all, v_all, c_refs, b_refs, bias_ref, lowest, 0, kv_heads)
    mark = token_marks(rows, width)
    scale = jnp.exp2(sc_ref[...].astype(f32))
    for head in range(here):
        cols = pl.ds(head * width, width)
        qd[:, cols] = decoded(q_ref[:, cols], scale, (first + head) * (width // BLOCK))
    steps = here // group
    s = product(blocks_of(qd, group, 0, width, mark), k_all[0])
    for step in range(steps):
        g = (first + step * group) // per_kv - lowest
        later = None
        if step + 1 < steps:
            later = product(blocks_of(qd, group, step + 1, width, mark), k_all[(first + (step + 1) * group) // per_kv - lowest])
        top = jnp.max(s, axis=1, keepdims=True)
        w = jnp.exp2((s - top) * factor)
        total = jnp.sum(w, axis=1, keepdims=True)
        at = pl.ds(step * group * rows, group * rows)
        acc[at, :] = jnp.dot(w.astype(bf16), v_all[g], preferred_element_type=f32)
        top_ref[at, :] = jnp.broadcast_to(top, (group * rows, width))
        total_ref[at, :] = jnp.broadcast_to(total, (group * rows, width))
        s = later


def late_kernel(*refs, cs, bs, parts, kv_heads, width, group, lead, skip):
    first_tokens = lax.axis_index("seq") == 0
    pl.when(first_tokens if lead else jnp.logical_not(first_tokens))(
        functools.partial(finish, refs, cs, bs, parts, kv_heads, width, group, skip)
    )


def finish(refs, cs, bs, parts, kv_heads, width, group, skip):
    bias_ref = refs[0]
    c_refs, b_refs = refs[1 : 1 + cs], refs[1 + cs : 1 + cs + bs]
    states = [refs[1 + cs + bs + 4 * n : 5 + cs + bs + 4 * n] for n in range(parts)]
    out_ref, k_all, v_all, staged, sem = refs[-5:]
    rows = staged.shape[0]
    per_kv = out_ref.shape[2] // width // kv_heads
    factor = math.log2(math.e) / math.sqrt(width)
    keys = k_all.shape[1]
    gather(k_all, v_all, c_refs, b_refs, bias_ref, 0, skip, kv_heads)
    mark = token_marks(rows, width)
    todo = []
    for state in states:
        for step in range(state[0].shape[1] // width // group):
            todo.append((state, step, len(todo) * group // per_kv))
    state, step, g = todo[0]
    s = product(blocks_of(state[0], group, step, width, mark), k_all[g])
    copies = []
    for n, (state, step, g) in enumerate(todo):
        later = None
        if n + 1 < len(todo):
            later = product(blocks_of(todo[n + 1][0][0], group, todo[n + 1][1], width, mark), k_all[todo[n + 1][2]])
        _, acc, top_ref, total_ref = state
        at = pl.ds(step * group * rows, group * rows)
        old = top_ref[at, :]
        top = jnp.maximum(old, jnp.broadcast_to(jnp.max(s, axis=1, keepdims=True), old.shape))
        keep = jnp.exp2((old - top) * factor)
        w = jnp.exp2((s - jnp.concatenate([top] * pl.cdiv(keys, width), axis=1)[:, :keys]) * factor)
        total = total_ref[at, :] * keep + jnp.sum(w, axis=1, keepdims=True)
        o = acc[at, :] * keep + jnp.dot(w.astype(bf16), v_all[g], preferred_element_type=f32)
        copies.append(send(staged, out_ref, sem, n, group, width, 0, (o / total).astype(bf16)))
        copies[-1].start()
        s = later
    for copy in copies:
        copy.wait()


def in_hbm(x):
    return pltpu.with_memory_space_constraint(x, pltpu.MemorySpace.HBM)


def natural(here, d):
    return jnp.int32(d)


def mirrored(here, d):
    return lax.bitwise_xor(here, d)


NEAR = [(0, 1), (1, 0), (2, 3), (3, 2)]
FAR = [(0, 2), (2, 0), (1, 3), (3, 1)]


def pick_natural(c_refs, b_refs):
    c, b = c_refs[0], b_refs[0]
    count = c.shape[0]
    kv_heads = c.shape[1] // 2
    keys = [lambda g, d=d: c[d, g] for d in range(count)]
    values = [lambda g, d=d: c[d, kv_heads + g] for d in range(count)]
    return keys, values, [b.at[d] for d in range(count)]


def pick_mirrored(c_refs, b_refs):
    kv_heads = c_refs[0].shape[0] // 2
    keys = [lambda g, c=c: c[g] for c in c_refs]
    values = [lambda g, c=c: c[kv_heads + g] for c in c_refs]
    return keys, values, b_refs


def body(q_mant, q_scale, key_m, key_e, value_m, value_e, cached_k, cached_v, start):
    _, rows, features = q_mant.shape
    _, kv_heads, held, width = cached_k.shape
    count = lax.axis_size("seq")
    sections = lax.axis_size("section")
    heads = features // width
    keys = count * (held + rows)
    mirror = count == len(NEAR)
    slots = range(count)
    if mirror:
        early, late = slots[:-1], slots[-1:]
        early_b, late_b = slots[0::2], slots[1::2]
    else:
        early, late, early_b, late_b = slots, (), slots, ()
    pieces = [(cached, d) for part in ((early, early_b), (late, late_b)) for cached, group in zip((True, False), part) for d in group]
    sizes = [heads * n // sum(SHARES) for n in SHARES]
    kv, cached, *q = pl.pallas_call(
        functools.partial(first_kernel, width=width),
        out_shape=(
            jax.ShapeDtypeStruct((rows, 2 * kv_heads * width + q_scale.shape[2]), bf16),
            jax.ShapeDtypeStruct((2 * kv_heads, held, width), bf16),
            *(jax.ShapeDtypeStruct((rows, n * width), bf16) for n in sizes),
        ),
        in_specs=[HBM] * 8,
        out_specs=(VMEM,) * (2 + len(sizes)),
        scratch_shapes=[
            pltpu.VMEM(q_scale.shape[1:], jnp.int32),
            pltpu.VMEM(key_m.shape[1:], bf16),
            pltpu.VMEM((key_e.shape[2], rows), jnp.int32),
            pltpu.VMEM(value_m.shape[1:], bf16),
            pltpu.VMEM((value_e.shape[2], rows), jnp.int32),
            pltpu.SemaphoreType.DMA((7 + len(sizes),)),
        ],
        compiler_params=pltpu.CompilerParams(vmem_limit_bytes=8 << 20),
        name="first",
    )(*(
        in_hbm(x)
        for x in (q_mant, q_scale, key_m, jnp.swapaxes(key_e, 1, 2), value_m, jnp.swapaxes(value_e, 1, 2), cached_k, cached_v)
    ))
    limits = jnp.broadcast_to(start.reshape(1, 1), (8, width))
    bias = pl.pallas_call(
        functools.partial(bias_kernel, pieces=pieces, held=held, rows=rows, source=mirrored if mirror else natural),
        out_shape=jax.ShapeDtypeStruct((keys, width), bf16),
        in_specs=[VMEM],
        out_specs=VMEM,
        compiler_params=pltpu.CompilerParams(vmem_limit_bytes=8 << 20),
        name="bias",
    )(limits)
    relay = [(i, (i + 1) % sections) for i in range(sections)]
    kv = lax.ppermute(kv, "section", relay)
    kv, scale = kv[:, : 2 * kv_heads * width], kv[:, 2 * kv_heads * width :]
    q = [lax.ppermute(x, "section", relay) for x in q]
    if mirror:
        near = lax.ppermute(cached, "seq", NEAR)
        far = lax.ppermute(cached, "seq", FAR)
        c = [cached, near, far, lax.ppermute(far, "seq", NEAR)]
        far = lax.ppermute(kv, "seq", FAR)
        near = lax.ppermute(kv, "seq", NEAR)
        b = [kv, far, near, lax.ppermute(far, "seq", NEAR)]
    else:
        c = [lax.all_gather(cached, "seq", axis=0)]
        b = [lax.all_gather(kv, "seq", axis=0)]
    group = 4
    limit = (8 << 20) + keys * width * kv_heads * 8 + keys * group * rows * 12 + 4 * rows * features
    if mirror:
        first, states = 0, []
        most = len(early) * held + len(early_b) * rows
        whole = pl.cdiv(most, width) * width
        for x, n in zip(q, sizes):
            held_heads = max(1, n * kv_heads // heads)
            call = pl.pallas_call(
                functools.partial(
                    early_kernel, cs=len(early), bs=len(early_b), heads=heads, kv_heads=kv_heads, width=width, group=2 * group, first=first
                ),
                out_shape=(jax.ShapeDtypeStruct((rows, n * width), bf16),) + (jax.ShapeDtypeStruct((n * rows, width), f32),) * 3,
                in_specs=[VMEM] * (3 + len(early) + len(early_b)),
                out_specs=(VMEM,) * 4,
                scratch_shapes=[pltpu.VMEM((held_heads, whole, 2 * width), bf16), pltpu.VMEM((held_heads, whole, width), bf16)],
                compiler_params=pltpu.CompilerParams(vmem_limit_bytes=limit),
                name="early",
            )
            states += call(x, scale, bias, *c[: len(early)], *b[: len(early_b)])
            first += n
        out = []
        for lead in (True, False):
            blocks = [] if lead else b[len(early_b) :]
            fresh = len(late) * held + len(blocks) * rows
            padded = pl.cdiv(fresh, width) * width
            call = pl.pallas_call(
                functools.partial(
                    late_kernel,
                    cs=len(late),
                    bs=len(blocks),
                    parts=len(sizes),
                    kv_heads=kv_heads,
                    width=width,
                    group=2 * group,
                    lead=lead,
                    skip=most,
                ),
                out_shape=jax.ShapeDtypeStruct((1, rows, features), bf16),
                in_specs=[VMEM] * (1 + len(late) + len(blocks) + len(states)) + [pl.BlockSpec(memory_space=pl.ANY)] * len(out),
                out_specs=pl.BlockSpec(memory_space=pl.ANY),
                scratch_shapes=[
                    pltpu.VMEM((kv_heads, padded, 2 * width), bf16),
                    pltpu.VMEM((kv_heads, padded, width), bf16),
                    pltpu.VMEM((rows, features), bf16),
                    pltpu.SemaphoreType.DMA((heads // group,)),
                ],
                input_output_aliases={} if lead else {1 + len(late) + len(blocks) + len(states): 0},
                compiler_params=pltpu.CompilerParams(vmem_limit_bytes=limit),
                name="late",
            )
            out = [call(bias, *c[len(early) :], *blocks, *states, *out)]
        return out[0]
    out, first = (), 0
    for x, n in zip(q, sizes):
        held_heads = max(1, n * kv_heads // heads)
        out = (
            pl.pallas_call(
                functools.partial(
                    attend_kernel,
                    cs=len(c),
                    bs=len(b),
                    pick=pick_mirrored if mirror else pick_natural,
                    kv_heads=kv_heads,
                    width=width,
                    group=group,
                    first=first,
                ),
                out_shape=jax.ShapeDtypeStruct((1, rows, features), bf16),
                in_specs=[VMEM] * (3 + len(c) + len(b)) + [pl.BlockSpec(memory_space=pl.ANY)] * len(out),
                out_specs=pl.BlockSpec(memory_space=pl.ANY),
                scratch_shapes=[
                    pltpu.VMEM((held_heads, keys, 2 * width), bf16),
                    pltpu.VMEM((held_heads, keys, width), bf16),
                    pltpu.VMEM((rows, n * width), bf16),
                    pltpu.SemaphoreType.DMA((n // group,)),
                ],
                input_output_aliases={3 + len(c) + len(b): 0} if out else {},
                compiler_params=pltpu.CompilerParams(vmem_limit_bytes=limit),
            )(x, scale, bias, *c, *b, *out),
        )
        first += n
    return out[0]


SHARES = (1, 1)


def solution(mesh):
    rows = P("section", "seq", "tensor")

    step = jax.shard_map(
        body,
        mesh=mesh,
        in_specs=(rows,) * 6 + (P("section", "tensor", "seq", None),) * 2 + (P("section"),),
        out_specs=rows,
        check_vma=False,
    )
    if mesh.shape["seq"] != len(NEAR):
        return step
    return step
```
